768 devices in a mesh: rows: 64 (over y, x, core), cols: 12 (over z).
Axes of the slice: x: 4, y: 8, z: 12, core: 2. Of those that a mesh axis runs over, the one named last changes fastest.
Arguments:
- known_inverse: bfloat16 [12, 64, 32, 24576], P(None, 'rows', None, 'cols'), may hold values from -6 to 6
- lower_panel: bfloat16 [4, 12, 64, 32, 512], P(None, 'cols'), may hold values from -0.0390625 to 0.0390625
- chain_panel: bfloat16 [4, 512, 512], replicated, may hold values from -0.25 to 0.25
- diag_inverse: float32 [4, 512, 512], P(None, 'rows'), may hold values from -6 to 6
- top_cols: bfloat16 [12, 64, 32, 512], P('cols', 'rows'), may hold values from -6 to 6
- top_diag: float32 [512, 512], P('rows'), may hold values from -6 to 6
- pattern: int32 [4, 768], replicated, may hold values from 0 to 1, as said below
Outputs:
- inverse_cols: bfloat16 [4, 12, 64, 32, 512], P(None, 'cols', 'rows')
- inverse_diag: float32 [4, 512, 512], P(None, 'rows')
- inverse_sub: float32 [4, 512, 512], P(None, 'rows')
The draws below stay inside these ranges and needn't reach their ends.
Inputs may be any that keep to these rules, and one draw needn't show every extreme that they name: `pattern`: row k marks exactly (768 * (5 + k)) // 9 block rows, and every block row marked in row k is marked in row k + 1.
All inputs are finite; a program needn't handle non-finite values.
Results may differ from the reference program's by a relative error of at most 0.025.
Values may be sent and summed in bfloat16 or wider, within the bound.
A program may use at most 128 MiB of HBM per device.

```python
import jax
import jax.numpy as jnp
from jax import lax

W = 512
PIECE = 32
SUPERS = 4
NU = 24576
N_ROWS = 64
N_COLS = 12


def draw_pattern(key, part):
    total = N_COLS * N_ROWS
    ranking = jax.random.permutation(key, total)
    section = jnp.arange(SUPERS, dtype=jnp.int32)
    marked = total * (SUPERS + 1 + section) // (2 * SUPERS + 1)
    return (ranking[None, :] < marked[:, None]).astype(jnp.int32)


def levels(rng, shape, shards, low, high):
    loudness, own = 1.0, jax.random.fold_in(rng, 6)
    for axis_at, shards_of in shards:
        heights = jnp.exp(jax.random.uniform(jax.random.fold_in(own, axis_at), (shards_of,), jnp.float32, low / len(shards), high / len(shards)))
        loudness = loudness * jnp.repeat(heights, shape[axis_at] // shards_of).reshape([-1 if axis == axis_at else 1 for axis in range(len(shape))])
    return loudness


def noise(stream_key, dims, deviation, reach, split=(), kind=jnp.bfloat16):
    factor_of = levels(stream_key, dims, split, -0.22, 0.18) if split else 1.0
    drawn = jax.random.normal(stream_key, dims, jnp.float32) * deviation * factor_of
    return jnp.minimum(jnp.maximum(drawn, -reach), reach).astype(kind)


def setup_inputs(seed: int = 0) -> dict:
    key_list = jax.random.split(jax.random.key(seed), 8)
    known_inverse = noise(key_list[0], (N_COLS, N_ROWS, PIECE, NU), 1.0, 6.0, ((1, 64), (3, 12)))
    lower_panel = noise(key_list[1], (SUPERS, N_COLS, N_ROWS, PIECE, W), NU ** -0.5, 0.0390625, ((1, 12),))
    chain_panel = noise(key_list[2], (SUPERS, W, W), W ** -0.5, 0.25)
    diag_inverse = noise(key_list[3], (SUPERS, W, W), 1.0, 6.0, ((1, 64),), jnp.float32)
    top_cols = noise(key_list[4], (N_COLS, N_ROWS, PIECE, W), 1.0, 6.0, ((0, 12), (1, 64)))
    top_diag = noise(key_list[5], (W, W), 1.0, 6.0, ((0, 64),), jnp.float32)
    pattern = draw_pattern(jax.random.fold_in(key_list[7], 71), 0)
    return dict(known_inverse=known_inverse, lower_panel=lower_panel, chain_panel=chain_panel, diag_inverse=diag_inverse, top_cols=top_cols, top_diag=top_diag, pattern=pattern)


def reference(known_inverse, lower_panel, chain_panel, diag_inverse, top_cols, top_diag, pattern):
    order = N_COLS * N_ROWS * PIECE
    ancestor = known_inverse.reshape(order, order)
    block_mask = pattern.astype(jnp.bfloat16)
    masked_panel = (lower_panel.reshape(SUPERS, N_COLS * N_ROWS, PIECE, W) * block_mask[:, :, None, None]).reshape(SUPERS, order, W)
    stacked = jnp.transpose(masked_panel, (1, 0, 2)).reshape(order, SUPERS * W)
    col_span = order // N_COLS
    running = jnp.zeros((order, SUPERS * W), jnp.float32)
    for column in range(N_COLS):
        part_cols = ancestor[:, column * col_span:(column + 1) * col_span]
        part_rows = stacked[column * col_span:(column + 1) * col_span]
        rounded = jnp.dot(part_cols, part_rows, preferred_element_type=jnp.float32).astype(jnp.bfloat16)
        rounded = lax.optimization_barrier(rounded)
        running = running + rounded.astype(jnp.float32)
    product_all = running.reshape(order, SUPERS, W)
    prev_cols = top_cols.reshape(order, W)
    prev_diag = top_diag
    cols_list = [None] * SUPERS
    diag_list = [None] * SUPERS
    sub_list = [None] * SUPERS
    for section in reversed(range(SUPERS)):
        link_block = chain_panel[section]
        link_wide = link_block.astype(jnp.float32)
        row_mask = jnp.repeat(pattern[section].astype(jnp.float32), PIECE)
        carried = jnp.dot(prev_cols, link_block, preferred_element_type=jnp.float32)
        new_cols = (-(product_all[:, section] + carried) * row_mask[:, None]).astype(jnp.bfloat16)
        sub_block = -(jnp.dot(prev_cols.T, masked_panel[section], preferred_element_type=jnp.float32)
                      + jnp.dot(prev_diag, link_wide, precision=lax.Precision.HIGHEST))
        diag_block = (diag_inverse[section]
                      - jnp.dot(masked_panel[section].T, new_cols, preferred_element_type=jnp.float32)
                      - jnp.dot(link_wide.T, sub_block, precision=lax.Precision.HIGHEST))
        cols_list[section] = new_cols.reshape(N_COLS, N_ROWS, PIECE, W)
        diag_list[section] = diag_block
        sub_list[section] = sub_block
        prev_cols = new_cols
        prev_diag = diag_block
    return jnp.stack(cols_list), jnp.stack(diag_list), jnp.stack(sub_list)
```

```python
import functools

import jax
import jax.numpy as jnp
from jax import lax
from jax.experimental import pallas as pl
from jax.experimental.pallas import tpu as pltpu
from jax.sharding import PartitionSpec as P

BF = jnp.bfloat16
F32 = jnp.float32
MESH = pl.DeviceIdType.MESH
SUP = 4


def mm(a, b):
    return jnp.dot(a, b, preferred_element_type=F32)


def mm_t(a, b):
    return lax.dot_general(a, b, (((1,), (1,)), ((), ())), preferred_element_type=F32)


def fold(x):
    half = x.shape[1] // 2
    return jnp.concatenate([x[:, :half], x[:, half:]], axis=0)


def unfold(x):
    rows = x.shape[0] // 2
    return jnp.concatenate([x[:rows], x[rows:]], axis=1)


def kernel(nz, ny, nx, g_h, m_h, l_h, d_h, top_h, td_h, ml_h, pat, cols_h, diag_h, sub_h,
           gv, mv, lv, dv, topv, mlv, pv, rss, rsr, s1, r1, s2, zb, ds, da, fs, fr, tz, ts, tr,
           us, ur, ags, agr, nout, dout, sout,
           in_sem, out_sem, rs_ss, rs_rs, a1_ss, a1_rs, a2_ss, a2_rs, da_ss, da_rs, db_ss, db_rs,
           f_ss, f_rs, t_ss, t_rs, u_ss, u_rs, g_ss, g_rs):
    row = lax.axis_index("rows")
    c = lax.axis_index("cols")
    y = row // nx
    xc = row % nx
    pe = topv.shape[0]
    w = topv.shape[1]
    dc = w // (ny * nx)
    mp = 12 // nz
    seg = nx * pe

    def load(i, src, dst):
        return pltpu.make_async_copy(src, dst, in_sem.at[i])

    loads = {
        "g": load(0, g_h, gv), "ml": load(1, ml_h, mlv), "top": load(2, top_h, topv),
        "d": load(3, d_h, dv.at[pl.ds(0, 4)]), "td": load(4, td_h, dv.at[4]),
    }
    for k in range(SUP):
        loads["m%d" % k] = load(5 + k, m_h.at[k], mv.at[k])
        loads["l%d" % k] = load(9 + k, l_h.at[k], lv.at[k])
    for name in ("ml", "g", "m3", "m2", "m1", "m0", "top", "l3", "l2", "l1", "l0", "d", "td"):
        loads[name].start()

    def rcopy(src, dst, ss, rs, trow, tcol):
        return pltpu.make_async_remote_copy(src_ref=src, dst_ref=dst, send_sem=ss, recv_sem=rs,
                                            device_id=(trow, tcol), device_id_type=MESH)

    def xrow(p):
        return y * nx + (xc + p) % nx

    def yrow(p):
        return ((y + p) % ny) * nx + xc

    bar = pltpu.get_barrier_semaphore()

    def sig(trow, tcol):
        pl.semaphore_signal(bar, inc=1, device_id=(trow, tcol), device_id_type=MESH)

    def over(n, f):
        def body(p, carry):
            f(p)
            return carry
        lax.fori_loop(1, n, body, 0)

    over(nx, lambda p: sig(xrow(p), c))
    over(ny, lambda p: sig(yrow(p), c))
    over(nz, lambda p: sig(row, (c + p) % nz))
    tz[...] = jnp.zeros_like(tz)
    pl.semaphore_wait(bar, (nx - 1) + (ny - 1) + (nz - 1))

    hi, lo = nz // 2, (nz - 1) // 2

    def hops(k, d):
        return lo + (k + d) % 2 if hi != lo else hi

    def rs_copy(k, d, s):
        to = (c + 1) % nz if d == 0 else (c + nz - 1) % nz
        return rcopy(rss.at[k, d, s], rsr.at[k, d, s], rs_ss.at[k, d, s], rs_rs.at[k, d, s], row, to)

    def rs_dest(k, d, s):
        h = hops(k, d) - s
        return (c + h) % nz if d == 0 else (c + nz - h) % nz

    def rs_step(k, d, s):
        val = pv[k, rs_dest(k, d, s)]
        if s > 0:
            rs_copy(k, d, s - 1).wait_recv()
            val = val + rsr[k, d, s - 1].astype(F32)
        rss[k, d, s] = val.astype(BF)
        rs_copy(k, d, s).start()

    loads["ml"].wait()
    loads["g"].wait()

    def first(kk, carry):
        k = 3 - kk
        pltpu.make_async_copy(m_h.at[k], mv.at[k], in_sem.at[5 + k]).wait()
        lhs = gv[...] * mlv[pl.ds(k, 1), :].astype(BF)
        pv[k] = mm(lhs, mv[k]).reshape(nz, pe, w)
        rs_step(k, 0, 0)
        rs_step(k, 1, 0)
        return carry

    lax.fori_loop(0, SUP, first, 0)

    for name in ("top", "l3", "l2", "l1", "l0", "d", "td"):
        loads[name].wait()

    ysrc = c % ny
    ds[...] = jnp.concatenate([dv[4], dv[3], dv[2], dv[1]], axis=0).astype(BF)

    def da_copy(p):
        return rcopy(ds, da.at[xc], da_ss.at[p], da_rs, yrow(p), c)

    @pl.when(y == ysrc)
    def _():
        over(ny, lambda p: da_copy(p).start())
        da[xc] = ds[...]

    def a1_copy(g, p):
        return rcopy(s1.at[g, (xc + p) % nx], r1.at[g, xc], a1_ss.at[g, p], a1_rs.at[g, p], xrow(p), c)

    def a1_wait(g, p):
        src = (xc + nx - p) % nx
        rcopy(s1.at[g, src], r1.at[g, src], a1_ss.at[g, p], a1_rs.at[g, p], xrow(p), c).wait_recv()

    def a2_copy(g, p):
        return rcopy(s2.at[g, (y + p) % ny], zb.at[g, :, pl.ds(pl.multiple_of(y * seg, seg), seg)],
                     a2_ss.at[g, p], a2_rs.at[g, p], yrow(p), c)

    def a2_wait(g, p):
        src = (y + ny - p) % ny
        rcopy(s2.at[g, src], zb.at[g, :, pl.ds(pl.multiple_of(src * seg, seg), seg)],
              a2_ss.at[g, p], a2_rs.at[g, p], yrow(p), c).wait_recv()

    def stage1(g, arrays):
        stack = jnp.concatenate(arrays, axis=0)
        t = stack.T.reshape(ny, nx, dc, 4 * pe)
        for q in range(nx):
            s1[g, q] = t[:, q].reshape(ny * dc, 4 * pe).astype(BF)
        over(nx, lambda p: a1_copy(g, p).start())
        r1[g, xc] = s1[g, xc]

    lane_block = lax.broadcasted_iota(jnp.int32, (ny * dc, 4 * pe), 1) // pe

    def stage2(g):
        over(nx, lambda p: a1_wait(g, p))
        for h in range(nx // 4):
            x = [r1[g, 4 * h + q].astype(F32) for q in range(4)]
            outs = []
            for t in range(4):
                acc = None
                for q in range(4):
                    sh = (pe * (q - t)) % (4 * pe)
                    v = pltpu.roll(x[q], sh, 1) if sh else x[q]
                    acc = v if acc is None else jnp.where(lane_block == q, v, acc)
                outs.append(acc.reshape(ny, dc, 4 * pe))
            both = jnp.stack(outs, axis=1).reshape(ny, 4 * dc, 4 * pe)
            s2[g, :, :, 4 * pe * h:4 * pe * (h + 1)] = both.astype(BF)
        over(ny, lambda p: a2_copy(g, p).start())
        zb[g, :, pl.ds(pl.multiple_of(y * seg, seg), seg)] = s2[g, y]

    top = topv[...]
    b43 = mm(top, lv[3])
    b42 = mm(b43.astype(BF), lv[2])
    b41 = mm(b42.astype(BF), lv[1])
    b40 = mm(b41.astype(BF), lv[0])
    stage1(0, [b43, b42, b41, b40])

    def rs_tick(s):
        def body(kk, carry):
            k = 3 - kk
            rs_step(k, 0, s)
            rs_step(k, 1, s)
            return carry
        lax.fori_loop(0, SUP, body, 0)

    def db_copy(p):
        return rcopy(da.at[xc], da.at[xc], db_ss.at[p], db_rs.at[p], xrow(p), c)

    def db_wait(p):
        src = (xc + nx - p) % nx
        rcopy(da.at[src], da.at[src], db_ss.at[p], db_rs.at[p], xrow(p), c).wait_recv()

    state = {}

    def extra_a():
        @pl.when(y != ysrc)
        def _():
            rcopy(ds, da.at[xc], da_ss.at[0], da_rs, row, c).wait_recv()
        over(nx, lambda p: db_copy(p).start())

    def extra_b():
        stage2(0)

    def extra_c():
        eye = (lax.broadcasted_iota(jnp.int32, (dc, w), 1)
               == row * dc + lax.broadcasted_iota(jnp.int32, (dc, w), 0)).astype(F32)
        cur = []
        lefts = {}
        for j in range(1, 5):
            stack = jnp.concatenate([eye] + cur, axis=0).astype(BF)
            res = mm_t(stack, lv[j - 1])
            cur = [res[dc * i:dc * (i + 1)] for i in range(j)]
            lefts[j] = res
        state["lefts"] = lefts

    def extra_d():
        over(nx, db_wait)
        src_row = lax.broadcasted_iota(jnp.int32, (w, nx * 4 * dc), 0)
        lane = lax.broadcasted_iota(jnp.int32, (w, nx * 4 * dc), 1)
        want = (ysrc * nx + lane // (4 * dc)) * dc + lane % dc
        own = lane // dc % 4
        parts = []
        for j in range(4, 0, -1):
            pick = jnp.where((src_row == want) & (own == 4 - j), 1.0, 0.0).astype(BF)
            parts.append(mm(state["lefts"][j].astype(BF), pick))
        full = jnp.concatenate(parts, axis=0).astype(BF)
        dx = mm(full, da[...].reshape(nx * 4 * dc, w))
        state["dx"] = jnp.where(c < ny, dx, 0.0)

    extras = [extra_a, extra_b, extra_c, extra_d]
    for s in range(1, hi):
        if lo > s or hi == lo:
            rs_tick(s)
        else:
            for k in (3, 2, 1, 0):
                for d in range(2):
                    if s < hops(k, d):
                        rs_step(k, d, s)
        if extras:
            extras.pop(0)()
    for f in extras:
        f()

    def product(k):
        out = pv[k, c]
        for d in range(2):
            h = hops(k, d)
            if h > 0:
                rs_copy(k, d, h - 1).wait_recv()
                out = out + rsr[k, d, h - 1].astype(F32)
        return out

    def finish(k, carried):
        own_mask = pat[k, c * (ny * nx) + row].astype(F32)
        new = (-(product(k) + carried) * own_mask).astype(BF)
        nout[k] = new
        return new

    n3 = finish(3, b43)
    b32 = mm(n3, lv[2])
    n2 = finish(2, b32)
    lev = mm(jnp.concatenate([b32.astype(BF), n2], axis=0), lv[1])
    b31, b21 = lev[:pe], lev[pe:]
    n1 = finish(1, b21)
    lev = mm(jnp.concatenate([b31.astype(BF), b21.astype(BF), n1], axis=0), lv[0])
    b30, b20, b10 = lev[:pe], lev[pe:2 * pe], lev[2 * pe:]
    stage1(1, [n3.astype(F32), b32, b31, b30])
    stage1(2, [n2.astype(F32), b21, b20, top.astype(F32)])
    n0 = finish(0, b10)
    stage1(3, [n1.astype(F32), b10, n0.astype(F32), jnp.zeros((pe, w), F32)])
    out_n = pltpu.make_async_copy(nout, cols_h, out_sem.at[0])
    out_n.start()
    stage2(1)
    stage2(2)
    stage2(3)

    def zmul(k, g0, g1):
        rows = 4 * dc * (g1 - g0)
        z = zb[g0:g1].reshape(rows, ny * seg)
        return mm(z * mlv[k:k + 1, :].astype(BF), mv[k])

    for g in range(3):
        over(ny, lambda p: a2_wait(g, p))
    o3 = zmul(3, 0, 3)
    o2 = zmul(2, 1, 3)
    over(ny, lambda p: a2_wait(3, p))
    o1 = zmul(1, 2, 4)
    o0 = zmul(0, 3, 4)

    def sl(o, i, n=1):
        return o[dc * i:dc * (i + n)]

    dx = state["dx"]
    zero = jnp.zeros((dc, w), F32)
    u = mm(sl(dx, 0, 4).astype(BF), lv[3]) + sl(o3, 0, 4)
    u = u + jnp.concatenate([zero, sl(dx, 4, 3)], axis=0)
    v = sl(o3, 4, 4)
    s3 = sl(o3, 11)
    w_u, w_v, w_s = [None] * 4, [None] * 4, [None] * 4
    w_u[3], w_v[3], w_s[3] = sl(u, 0), sl(v, 0), s3
    lev = mm(jnp.concatenate([sl(u, 1, 3), sl(v, 1, 3)], axis=0).astype(BF), lv[2])
    u = sl(lev, 0, 3) + sl(o2, 1, 3) + jnp.concatenate([zero, sl(dx, 7, 2)], axis=0)
    v = sl(lev, 3, 3) + sl(o2, 4, 3)
    w_u[2], w_v[2], w_s[2] = sl(u, 0), sl(v, 0), sl(o2, 0)
    lev = mm(jnp.concatenate([sl(u, 1, 2), sl(v, 1, 2)], axis=0).astype(BF), lv[1])
    u = sl(lev, 0, 2) + sl(o1, 1, 2) + jnp.concatenate([zero, sl(dx, 9, 1)], axis=0)
    v = sl(lev, 2, 2) + sl(o1, 4, 2)
    w_u[1], w_v[1], w_s[1] = sl(u, 0), sl(v, 0), sl(o1, 0)
    lev = mm(jnp.concatenate([sl(u, 1, 1), sl(v, 1, 1)], axis=0).astype(BF), lv[0])
    w_u[0] = sl(lev, 0) + sl(o0, 1)
    w_v[0] = sl(lev, 1) + sl(o0, 2)
    w_s[0] = sl(o0, 0)

    for k in range(SUP):
        fs[k] = fold(-w_v[k]).astype(BF)
        fs[4 + k] = fold(w_u[k]).astype(BF)
        fs[8 + k] = fold(w_s[k]).astype(BF)

    def f_copy(p):
        to = (c + p) % nz
        return rcopy(fs.at[pl.ds(to * mp, mp)], fr.at[c], f_ss.at[p], f_rs.at[p], row, to)

    def f_wait(p):
        src = (c + nz - p) % nz
        rcopy(fs.at[pl.ds(src * mp, mp)], fr.at[src], f_ss.at[p], f_rs.at[p], row, src).wait_recv()

    over(nz, lambda p: f_copy(p).start())
    fr[c] = fs[pl.ds(c * mp, mp)]
    over(nz, f_wait)
    total = jnp.sum(fr[...].astype(F32), axis=0)

    tl = tz.shape[0]
    off = pl.multiple_of((y % 2 * nx + xc) * dc, dc)
    for q in range(mp):
        tz[pl.ds(off, dc), :] = unfold(total[q])
        t = tz[...].T.reshape(ny, nx, dc, tl)
        for i in range(nx):
            ts[i, q] = t[:, i].reshape(ny * dc, tl).astype(BF)

    def t_copy(p):
        return rcopy(ts.at[(xc + p) % nx], tr.at[xc], t_ss.at[p], t_rs.at[p], xrow(p), c)

    def t_wait(p):
        src = (xc + nx - p) % nx
        rcopy(ts.at[src], tr.at[src], t_ss.at[p], t_rs.at[p], xrow(p), c).wait_recv()

    over(nx, lambda p: t_copy(p).start())
    tr[xc] = ts[xc]
    over(nx, t_wait)
    got = jnp.sum(tr[...].astype(F32), axis=0)
    for q in range(mp):
        us[:, q] = got[q].reshape(ny, dc, tl)

    def u_copy(p):
        return rcopy(us.at[(y + p) % ny], ur.at[y], u_ss.at[p], u_rs.at[p], yrow(p), c)

    def u_wait(p):
        src = (y + ny - p) % ny
        rcopy(us.at[src], ur.at[src], u_ss.at[p], u_rs.at[p], yrow(p), c).wait_recv()

    over(ny, lambda p: u_copy(p).start())
    ur[y] = us[y]
    over(ny, u_wait)
    for q in range(mp):
        flipped = jnp.concatenate([ur[2 * i, q] + ur[2 * i + 1, q] for i in range(ny // 2)], axis=1)
        ags[q] = jnp.where(c * mp + q < 4, fold(flipped), total[q]).astype(BF)

    def g_copy(p):
        return rcopy(ags, agr.at[pl.ds(c * mp, mp)], g_ss.at[p], g_rs.at[p], row, (c + p) % nz)

    def g_wait(p):
        src = (c + nz - p) % nz
        rcopy(ags, agr.at[pl.ds(src * mp, mp)], g_ss.at[p], g_rs.at[p], row, src).wait_recv()

    over(nz, lambda p: g_copy(p).start())
    agr[pl.ds(c * mp, mp)] = ags[...]
    over(nz, g_wait)

    for k in range(SUP):
        dout[k] = dv[k] + unfold(agr[k].astype(F32)) + unfold(agr[4 + k].astype(F32))
    for k in range(SUP):
        prev = dout[k + 1] if k < 3 else dv[4]
        big = prev.astype(BF)
        small = (prev - big.astype(F32)).astype(BF)
        both = mm(jnp.concatenate([big, small], axis=0), lv[k])
        sout[k] = -(unfold(agr[8 + k].astype(F32)) + both[:dc] + both[dc:])
    out_d = pltpu.make_async_copy(dout, diag_h, out_sem.at[1])
    out_s = pltpu.make_async_copy(sout, sub_h, out_sem.at[2])
    out_d.start()
    out_s.start()

    for s in range(hi):
        for k in range(SUP):
            for d in range(2):
                if s < hops(k, d):
                    rs_copy(k, d, s).wait_send()

    @pl.when(y == ysrc)
    def _():
        over(ny, lambda p: da_copy(p).wait_send())

    def drain_x(p):
        db_copy(p).wait_send()
        t_copy(p).wait_send()
        for g in range(4):
            a1_copy(g, p).wait_send()

    def drain_y(p):
        u_copy(p).wait_send()
        for g in range(4):
            a2_copy(g, p).wait_send()

    def drain_z(p):
        f_copy(p).wait_send()
        g_copy(p).wait_send()

    over(nx, drain_x)
    over(ny, drain_y)
    over(nz, drain_z)
    out_n.wait()
    out_d.wait()
    out_s.wait()


def local(known_inverse, lower_panel, chain_panel, diag_inverse, top_cols, top_diag, pattern):
    nr = lax.axis_size("rows")
    nz = lax.axis_size("cols")
    col = lax.axis_index("cols")
    nx = 8 if nr >= 64 else 4
    ny = nr // nx
    pe = known_inverse.shape[2]
    w = lower_panel.shape[-1]
    dc = w // nr
    mp = 12 // nz
    ub = nr * pe
    seg = nx * pe
    hi = nz // 2
    g = known_inverse.reshape(nz * pe, ub)
    m = lower_panel.reshape(SUP, ub, w)
    top = top_cols.reshape(pe, w)
    lanes = jnp.repeat(lax.dynamic_slice_in_dim(pattern, col * nr, nr, 1).astype(F32), pe, axis=1)
    tl = 2 * nx * dc
    dma = pltpu.SemaphoreType.DMA
    vm = pltpu.VMEM
    any_spec = pl.BlockSpec(memory_space=pl.ANY)
    scratch = [
        vm((nz * pe, ub), BF), vm((SUP, ub, w), BF), vm((SUP, w, w), BF), vm((SUP + 1, dc, w), F32),
        vm((pe, w), BF), vm((SUP, ub), F32), vm((SUP, nz, pe, w), F32),
        vm((SUP, 2, hi, pe, w), BF), vm((SUP, 2, hi, pe, w), BF),
        vm((4, nx, ny * dc, 4 * pe), BF), vm((4, nx, ny * dc, 4 * pe), BF),
        vm((4, ny, 4 * dc, seg), BF), vm((4, 4 * dc, ub), BF),
        vm((4 * dc, w), BF), vm((nx, 4 * dc, w), BF),
        vm((12, 2 * dc, w // 2), BF), vm((nz, mp, 2 * dc, w // 2), BF),
        vm((tl, w), F32), vm((nx, mp, ny * dc, tl), BF), vm((nx, mp, ny * dc, tl), BF),
        vm((ny, mp, dc, tl), F32), vm((ny, mp, dc, tl), F32),
        vm((mp, 2 * dc, w // 2), BF), vm((12, 2 * dc, w // 2), BF),
        vm((SUP, pe, w), BF), vm((SUP, dc, w), F32), vm((SUP, dc, w), F32),
        dma((13,)), dma((3,)), dma((SUP, 2, hi)), dma((SUP, 2, hi)),
        dma((4, nx)), dma((4, nx)), dma((4, ny)), dma((4, ny)),
        dma((ny,)), dma(()), dma((nx,)), dma((nx,)),
        dma((nz,)), dma((nz,)), dma((nx,)), dma((nx,)), dma((ny,)), dma((ny,)), dma((nz,)), dma((nz,)),
    ]
    cols, diag, sub = pl.pallas_call(
        functools.partial(kernel, nz, ny, nx),
        out_shape=(
            jax.ShapeDtypeStruct((SUP, pe, w), BF),
            jax.ShapeDtypeStruct((SUP, dc, w), F32),
            jax.ShapeDtypeStruct((SUP, dc, w), F32),
        ),
        in_specs=[any_spec] * 7 + [pl.BlockSpec(memory_space=pltpu.SMEM)],
        out_specs=(any_spec,) * 3,
        scratch_shapes=scratch,
        compiler_params=pltpu.CompilerParams(
            collective_id=0, has_side_effects=True, vmem_limit_bytes=48 * 1024 * 1024
        ),
        name="chain",
    )(g, m, chain_panel, diag_inverse, top, top_diag, lanes, pattern)
    return cols.reshape(SUP, 1, 1, pe, w), diag, sub


def solution(mesh):
    in_specs = (
        P(None, "rows", None, "cols"),
        P(None, "cols", None, None, None),
        P(),
        P(None, "rows", None),
        P("cols", "rows", None, None),
        P("rows", None),
        P(),
    )
    out_specs = (P(None, "cols", "rows", None, None), P(None, "rows", None), P(None, "rows", None))
    return jax.shard_map(local, mesh=mesh, in_specs=in_specs, out_specs=out_specs, check_vma=False)
```

```python
import functools

import jax
import jax.numpy as jnp
from jax import lax
from jax.experimental import pallas as pl
from jax.experimental.pallas import tpu as pltpu
from jax.sharding import PartitionSpec as P

BF = jnp.bfloat16
F32 = jnp.float32
MESH = pl.DeviceIdType.MESH
SUP = 4
OFF = {3: 0, 2: 1, 1: 2, 0: 3}


def mm(a, b):
    return jnp.dot(a, b, preferred_element_type=F32)


def mm_t(a, b):
    return lax.dot_general(a, b, (((1,), (1,)), ((), ())), preferred_element_type=F32)


def fold(x):
    half = x.shape[1] // 2
    return jnp.concatenate([x[:, :half], x[:, half:]], axis=0)


def unfold(x):
    rows = x.shape[0] // 2
    return jnp.concatenate([x[:rows], x[rows:]], axis=1)


def plane_w(k, nz):
    return (3 * k) % nz


def plane_s(k, nz):
    return (3 * k + 1) % nz


def kernel(nz, ny, nx, g_h, m_h, l_h, d_h, top_h, td_h, pat, cols_h, diag_h, sub_h,
           gv, mv, lv, dv, topv, mlv, pv, rss, rsr, s1, r1, s2, zb, ds, da, fs, fr, fw, fv, tz, ts, tr,
           us, ur, gs, gw, ags, agw, nout, dout, sout,
           in_sem, out_sem, rs_ss, rs_rs, a1_ss, a1_rs, a2_ss, a2_rs, da_ss, da_rs, db_ss, db_rs,
           f_ss, f_rs, w_ss, w_rs, t_ss, t_rs, u_ss, u_rs, g_ss, g_rs, h_ss, h_rs):
    row = lax.axis_index("rows")
    c = lax.axis_index("cols")
    y = row // nx
    xc = row % nx
    pe = topv.shape[0]
    w = topv.shape[1]
    dc = w // (ny * nx)
    seg = nx * pe

    def load(i, src, dst):
        return pltpu.make_async_copy(src, dst, in_sem.at[i])

    loads = {
        "g": load(0, g_h, gv), "top": load(2, top_h, topv),
        "d": load(3, d_h, dv.at[pl.ds(0, 4)]), "td": load(4, td_h, dv.at[4]),
    }
    for k in range(SUP):
        loads["m%d" % k] = load(5 + k, m_h.at[k], mv.at[k])
        loads["l%d" % k] = load(9 + k, l_h.at[k], lv.at[k])
    loads["g"].start()
    loads["m3"].start()

    def rcopy(src, dst, ss, rs, trow, tcol):
        return pltpu.make_async_remote_copy(src_ref=src, dst_ref=dst, send_sem=ss, recv_sem=rs,
                                            device_id=(trow, tcol), device_id_type=MESH)

    def xrow(p):
        return y * nx + (xc + p) % nx

    def yrow(p):
        return ((y + p) % ny) * nx + xc

    bar = pltpu.get_barrier_semaphore()

    def sig(trow, tcol):
        pl.semaphore_signal(bar, inc=1, device_id=(trow, tcol), device_id_type=MESH)

    def over(n, f):
        def body(p, carry):
            f(p)
            return carry
        lax.fori_loop(1, n, body, 0)

    over(nx, lambda p: sig(xrow(p), c))
    over(ny, lambda p: sig(yrow(p), c))
    over(nz, lambda p: sig(row, (c + p) % nz))
    lane = lax.broadcasted_iota(jnp.int32, (1, 128), 1) // pe

    def mask_lanes(v, carry):
        for k in range(SUP):
            val = jnp.zeros((1, 128), F32)
            for q in range(128 // pe):
                one = pat[k, c * (ny * nx) + v * (128 // pe) + q].astype(F32)
                val = jnp.where(lane == q, one, val)
            mlv[pl.ds(k, 1), pl.ds(pl.multiple_of(v * 128, 128), 128)] = val
        return carry

    lax.fori_loop(0, ny * nx * pe // 128, mask_lanes, 0)
    tz[...] = jnp.zeros_like(tz)
    loads["g"].wait()
    pl.semaphore_wait(bar, (nx - 1) + (ny - 1) + (nz - 1))

    hi, lo = nz // 2, (nz - 1) // 2

    def hops(k, d):
        return lo + (k + d) % 2 if hi != lo else hi

    def rs_copy(k, d, s):
        to = (c + 1) % nz if d == 0 else (c + nz - 1) % nz
        return rcopy(rss.at[k, d, s], rsr.at[k, d, s], rs_ss.at[k, d, s], rs_rs.at[k, d, s], row, to)

    def rs_dest(k, d, s):
        h = hops(k, d) - s
        return (c + h) % nz if d == 0 else (c + nz - h) % nz

    def rs_step(k, d, s):
        val = pv[k, rs_dest(k, d, s)]
        if s > 0:
            rs_copy(k, d, s - 1).wait_recv()
            val = val + rsr[k, d, s - 1].astype(F32)
        rss[k, d, s] = val.astype(BF)
        rs_copy(k, d, s).start()

    def product_part(k):
        loads["m%d" % k].wait()
        for name in after[k]:
            loads[name].start()
        lhs = gv[...] * mlv[k:k + 1, :].astype(BF)
        pv[k] = mm(lhs, mv[k]).reshape(nz, pe, w)

    after = {3: ("m2", "top", "l3", "l2"), 2: ("m1", "l1", "l0"), 1: ("m0", "d", "td"), 0: ()}

    ysrc = c % ny
    def da_copy(p):
        return rcopy(ds, da.at[xc], da_ss.at[p], da_rs, yrow(p), c)

    def da_send():
        loads["d"].wait()
        loads["td"].wait()
        ds[...] = jnp.concatenate([dv[4], dv[3], dv[2], dv[1]], axis=0).astype(BF)

        @pl.when(y == ysrc)
        def _():
            over(ny, lambda p: da_copy(p).start())
            da[xc] = ds[...]

    def a1_copy(g, p):
        return rcopy(s1.at[g, (xc + p) % nx], r1.at[g, xc], a1_ss.at[g, p], a1_rs.at[g, p], xrow(p), c)

    def a1_wait(g, p):
        src = (xc + nx - p) % nx
        rcopy(s1.at[g, src], r1.at[g, src], a1_ss.at[g, p], a1_rs.at[g, p], xrow(p), c).wait_recv()

    def a2_copy(g, p):
        return rcopy(s2.at[g, (y + p) % ny], zb.at[g, :, pl.ds(pl.multiple_of(y * seg, seg), seg)],
                     a2_ss.at[g, p], a2_rs.at[g, p], yrow(p), c)

    def a2_wait(g, p):
        src = (y + ny - p) % ny
        rcopy(s2.at[g, src], zb.at[g, :, pl.ds(pl.multiple_of(src * seg, seg), seg)],
              a2_ss.at[g, p], a2_rs.at[g, p], yrow(p), c).wait_recv()

    def stage1(g, arrays):
        stack = jnp.concatenate(arrays, axis=0)
        t = stack.T.reshape(ny, nx, dc, 4 * pe)
        for q in range(nx):
            s1[g, q] = t[:, q].reshape(ny * dc, 4 * pe).astype(BF)
        over(nx, lambda p: a1_copy(g, p).start())
        r1[g, xc] = s1[g, xc]

    lane_block = lax.broadcasted_iota(jnp.int32, (ny * dc, 4 * pe), 1) // pe

    def stage2(g):
        over(nx, lambda p: a1_wait(g, p))
        for h in range(nx // 4):
            x = [r1[g, 4 * h + q].astype(F32) for q in range(4)]
            outs = []
            for t in range(4):
                acc = None
                for q in range(4):
                    sh = (pe * (q - t)) % (4 * pe)
                    v = pltpu.roll(x[q], sh, 1) if sh else x[q]
                    acc = v if acc is None else jnp.where(lane_block == q, v, acc)
                outs.append(acc.reshape(ny, dc, 4 * pe))
            both = jnp.stack(outs, axis=1).reshape(ny, 4 * dc, 4 * pe)
            s2[g, :, :, 4 * pe * h:4 * pe * (h + 1)] = both.astype(BF)
        over(ny, lambda p: a2_copy(g, p).start())
        zb[g, :, pl.ds(pl.multiple_of(y * seg, seg), seg)] = s2[g, y]

    state = {}

    def group0():
        for name in ("top", "l3", "l2", "l1", "l0"):
            loads[name].wait()
        b43 = mm(topv[...], lv[3])
        b42 = mm(b43.astype(BF), lv[2])
        b41 = mm(b42.astype(BF), lv[1])
        b40 = mm(b41.astype(BF), lv[0])
        state["b43"] = b43
        stage1(0, [b43, b42, b41, b40])

    def db_copy(p):
        return rcopy(da.at[xc], da.at[xc], db_ss.at[p], db_rs.at[p], xrow(p), c)

    def db_wait(p):
        src = (xc + nx - p) % nx
        rcopy(da.at[src], da.at[src], db_ss.at[p], db_rs.at[p], xrow(p), c).wait_recv()

    def extra_a():
        @pl.when(y != ysrc)
        def _():
            rcopy(ds, da.at[xc], da_ss.at[0], da_rs, row, c).wait_recv()
        over(nx, lambda p: db_copy(p).start())

    def extra_c():
        eye = (lax.broadcasted_iota(jnp.int32, (dc, w), 1)
               == row * dc + lax.broadcasted_iota(jnp.int32, (dc, w), 0)).astype(F32)
        cur = []
        lefts = {}
        for j in range(1, 5):
            stack = jnp.concatenate([eye] + cur, axis=0).astype(BF)
            res = mm_t(stack, lv[j - 1])
            cur = [res[dc * i:dc * (i + 1)] for i in range(j)]
            lefts[j] = res
        state["lefts"] = lefts

    def extra_d():
        over(nx, db_wait)
        src_row = lax.broadcasted_iota(jnp.int32, (w, nx * 4 * dc), 0)
        lane = lax.broadcasted_iota(jnp.int32, (w, nx * 4 * dc), 1)
        want = (ysrc * nx + lane // (4 * dc)) * dc + lane % dc
        own = lane // dc % 4
        parts = []
        for j in range(4, 0, -1):
            pick = jnp.where((src_row == want) & (own == 4 - j), 1.0, 0.0).astype(BF)
            parts.append(mm(state["lefts"][j].astype(BF), pick))
        full = jnp.concatenate(parts, axis=0).astype(BF)
        dx = mm(full, da[...].reshape(nx * 4 * dc, w))
        state["dx"] = jnp.where(c < ny, dx, 0.0)

    def product(k):
        out = pv[k, c]
        for d in range(2):
            h = hops(k, d)
            if h > 0:
                rs_copy(k, d, h - 1).wait_recv()
                out = out + rsr[k, d, h - 1].astype(F32)
        return out

    def finish(k, carried):
        own_mask = pat[k, c * (ny * nx) + row].astype(F32)
        new = (-(product(k) + carried) * own_mask).astype(BF)
        nout[k] = new
        return new

    def tail3():
        n3 = finish(3, state["b43"])
        b32 = mm(n3, lv[2])
        b31 = mm(b32.astype(BF), lv[1])
        b30 = mm(b31.astype(BF), lv[0])
        state["b32"] = b32
        stage1(1, [n3.astype(F32), b32, b31, b30])

    def tail2():
        n2 = finish(2, state["b32"])
        b21 = mm(n2, lv[1])
        b20 = mm(b21.astype(BF), lv[0])
        state["b21"] = b21
        stage1(2, [n2.astype(F32), b21, b20, topv[...].astype(F32)])

    def tail1():
        n1 = finish(1, state["b21"])
        state["n1"] = n1
        state["b10"] = mm(n1, lv[0])

    def tail0():
        n0 = finish(0, state["b10"])
        stage1(3, [state["n1"].astype(F32), state["b10"], n0.astype(F32), jnp.zeros((pe, w), F32)])

    hooks = {}

    def hook(t, f):
        hooks.setdefault(t, []).append(f)

    end = {k: OFF[k] + hi for k in range(SUP)}
    hook(2, group0)
    hook(3, da_send)
    hook(4, lambda: stage2(0))
    hook(4, extra_a)
    hook(4, extra_c)
    hook(5, extra_d)
    hook(end[3], tail3)
    hook(end[2], tail2)
    hook(max(end[2], end[3] + 1), lambda: stage2(1))
    hook(end[1], tail1)
    hook(end[0], tail0)
    for t in range(max(max(end.values()), max(hooks)) + 1):
        for k in range(SUP):
            if t == OFF[k]:
                product_part(k)
                rs_step(k, 0, 0)
                rs_step(k, 1, 0)
        for k in (3, 2, 1, 0):
            s = t - OFF[k]
            for d in range(2):
                if 0 < s < hops(k, d):
                    rs_step(k, d, s)
        for f in hooks.get(t, ()):
            f()
    out_n = pltpu.make_async_copy(nout, cols_h, out_sem.at[0])
    out_n.start()
    stage2(2)

    def zmul(k, g0, g1):
        rows = 4 * dc * (g1 - g0)
        z = zb[g0:g1].reshape(rows, ny * seg)
        return mm(z * mlv[k:k + 1, :].astype(BF), mv[k])

    for g in range(3):
        over(ny, lambda p: a2_wait(g, p))
    o3 = zmul(3, 0, 3)
    o2 = zmul(2, 1, 3)
    fs[3] = fold(o3[11 * dc:]).astype(BF)
    fs[2] = fold(o2[:dc]).astype(BF)

    def f_copy(k):
        return rcopy(fs.at[k], fr.at[c], f_ss.at[k], f_rs.at[c], row, plane_s(k, nz))

    def f_send(k):
        @pl.when(c != plane_s(k, nz))
        def _():
            f_copy(k).start()

        @pl.when(c == plane_s(k, nz))
        def _():
            fr[c] = fs[k]

    f_send(3)
    f_send(2)
    stage2(3)
    for s in range(hi):
        for k in range(SUP):
            for d in range(2):
                if s < hops(k, d):
                    rs_copy(k, d, s).wait_send()
    over(ny, lambda p: a2_wait(3, p))
    o1 = zmul(1, 2, 4)
    o0 = zmul(0, 3, 4)
    fs[1] = fold(o1[:dc]).astype(BF)
    fs[0] = fold(o0[:dc]).astype(BF)
    f_send(1)
    f_send(0)

    def sl(o, i, n=1):
        return o[dc * i:dc * (i + n)]

    dx = state["dx"]
    zero = jnp.zeros((dc, w), F32)
    u = mm(sl(dx, 0, 4).astype(BF), lv[3]) + sl(o3, 0, 4)
    u = u + jnp.concatenate([zero, sl(dx, 4, 3)], axis=0)
    v = sl(o3, 4, 4)
    w_u, w_v = [None] * 4, [None] * 4
    w_u[3], w_v[3] = sl(u, 0), sl(v, 0)
    lev = mm(jnp.concatenate([sl(u, 1, 3), sl(v, 1, 3)], axis=0).astype(BF), lv[2])
    u = sl(lev, 0, 3) + sl(o2, 1, 3) + jnp.concatenate([zero, sl(dx, 7, 2)], axis=0)
    v = sl(lev, 3, 3) + sl(o2, 4, 3)
    w_u[2], w_v[2] = sl(u, 0), sl(v, 0)
    lev = mm(jnp.concatenate([sl(u, 1, 2), sl(v, 1, 2)], axis=0).astype(BF), lv[1])
    u = sl(lev, 0, 2) + sl(o1, 1, 2) + jnp.concatenate([zero, sl(dx, 9, 1)], axis=0)
    v = sl(lev, 2, 2) + sl(o1, 4, 2)
    w_u[1], w_v[1] = sl(u, 0), sl(v, 0)
    lev = mm(jnp.concatenate([sl(u, 1, 1), sl(v, 1, 1)], axis=0).astype(BF), lv[0])
    w_u[0] = sl(lev, 0) + sl(o0, 1)
    w_v[0] = sl(lev, 1) + sl(o0, 2)

    for k in range(SUP):
        fw[k, 0] = fold(-w_v[k]).astype(BF)
        fw[k, 1] = fold(w_u[k]).astype(BF)

    def w_copy(k):
        return rcopy(fw.at[k], fv.at[c], w_ss.at[k], w_rs.at[c], row, plane_w(k, nz))

    for k in range(SUP):
        @pl.when(c != plane_w(k, nz))
        def _():
            w_copy(k).start()

        @pl.when(c == plane_w(k, nz))
        def _():
            fv[c] = fw[k]

    def from_plane(p):
        return (c + nz - p) % nz

    def g_copy(k, p):
        return rcopy(gs, ags.at[k], g_ss.at[p], g_rs.at[k], row, (c + p) % nz)

    def h_copy(k, p):
        return rcopy(gw, agw.at[k], h_ss.at[p], h_rs.at[k], row, (c + p) % nz)

    for k in range(SUP):
        @pl.when(c == plane_s(k, nz))
        def _():
            def f_wait(p):
                src = from_plane(p)
                rcopy(fs.at[k], fr.at[src], f_ss.at[k], f_rs.at[src], row, src).wait_recv()

            over(nz, f_wait)
            gs[...] = jnp.sum(fr[...].astype(F32), axis=0).astype(BF)
            over(nz, lambda p: g_copy(k, p).start())
            ags[k] = gs[...]

    tl = tz.shape[0]

    def t_copy(p):
        return rcopy(ts.at[(xc + p) % nx], tr.at[xc], t_ss.at[p], t_rs.at[p], xrow(p), c)

    def t_wait(p):
        src = (xc + nx - p) % nx
        rcopy(ts.at[src], tr.at[src], t_ss.at[p], t_rs.at[p], xrow(p), c).wait_recv()

    def u_copy(p):
        return rcopy(us.at[(y + p) % ny], ur.at[y], u_ss.at[p], u_rs.at[p], yrow(p), c)

    def u_wait(p):
        src = (y + ny - p) % ny
        rcopy(us.at[src], ur.at[src], u_ss.at[p], u_rs.at[p], yrow(p), c).wait_recv()

    is_w = c == plane_w(0, nz)
    for k in range(1, SUP):
        is_w = is_w | (c == plane_w(k, nz))

    @pl.when(is_w)
    def _():
        def w_wait(p):
            src = from_plane(p)
            rcopy(fw.at[0], fv.at[src], w_ss.at[0], w_rs.at[src], row, src).wait_recv()

        over(nz, w_wait)
        total = jnp.sum(fv[...].astype(F32), axis=0)
        off = pl.multiple_of((y % 2 * nx + xc) * dc, dc)
        tz[pl.ds(off, dc), :] = unfold(total[0])
        t = tz[...].T.reshape(ny, nx, dc, tl)
        for i in range(nx):
            ts[i] = t[:, i].reshape(ny * dc, tl).astype(BF)
        over(nx, lambda p: t_copy(p).start())
        tr[xc] = ts[xc]
        over(nx, t_wait)
        us[...] = jnp.sum(tr[...].astype(F32), axis=0).reshape(ny, dc, tl)
        over(ny, lambda p: u_copy(p).start())
        ur[y] = us[y]
        over(ny, u_wait)
        flipped = jnp.concatenate([ur[2 * i] + ur[2 * i + 1] for i in range(ny // 2)], axis=1)
        gw[...] = (fold(flipped) + total[1]).astype(BF)

    for k in range(SUP):
        @pl.when(c == plane_w(k, nz))
        def _():
            over(nz, lambda p: h_copy(k, p).start())
            agw[k] = gw[...]

    def drain_x(p):
        db_copy(p).wait_send()
        for g in range(4):
            a1_copy(g, p).wait_send()

    def drain_y(p):
        for g in range(4):
            a2_copy(g, p).wait_send()

    over(nx, drain_x)
    over(ny, drain_y)

    @pl.when(y == ysrc)
    def _():
        over(ny, lambda p: da_copy(p).wait_send())

    for k in range(SUP):
        @pl.when(c != plane_s(k, nz))
        def _():
            f_copy(k).wait_send()
            g_copy(k, 1).wait_recv()

        @pl.when(c != plane_w(k, nz))
        def _():
            w_copy(k).wait_send()

    for k in (3, 2, 1, 0):
        @pl.when(c != plane_w(k, nz))
        def _():
            h_copy(k, 1).wait_recv()

        dout[k] = dv[k] + unfold(agw[k].astype(F32))
    for k in range(SUP):
        prev = dout[k + 1] if k < 3 else dv[4]
        big = prev.astype(BF)
        small = (prev - big.astype(F32)).astype(BF)
        both = mm(jnp.concatenate([big, small], axis=0), lv[k])
        sout[k] = -(unfold(ags[k].astype(F32)) + both[:dc] + both[dc:])
    out_d = pltpu.make_async_copy(dout, diag_h, out_sem.at[1])
    out_s = pltpu.make_async_copy(sout, sub_h, out_sem.at[2])
    out_d.start()
    out_s.start()

    @pl.when(is_w)
    def _():
        over(nx, lambda p: t_copy(p).wait_send())
        over(ny, lambda p: u_copy(p).wait_send())
        over(nz, lambda p: h_copy(0, p).wait_send())

    for k in range(SUP):
        @pl.when(c == plane_s(k, nz))
        def _():
            over(nz, lambda p: g_copy(k, p).wait_send())

    out_n.wait()
    out_d.wait()
    out_s.wait()


def local(known_inverse, lower_panel, chain_panel, diag_inverse, top_cols, top_diag, pattern):
    nr = lax.axis_size("rows")
    nz = lax.axis_size("cols")
    nx = 8 if nr >= 64 else 4
    ny = nr // nx
    pe = known_inverse.shape[2]
    w = lower_panel.shape[-1]
    dc = w // nr
    ub = nr * pe
    seg = nx * pe
    hi = nz // 2
    g = known_inverse.reshape(nz * pe, ub)
    m = lower_panel.reshape(SUP, ub, w)
    top = top_cols.reshape(pe, w)
    tl = 2 * nx * dc
    dma = pltpu.SemaphoreType.DMA
    vm = pltpu.VMEM
    any_spec = pl.BlockSpec(memory_space=pltpu.HBM)
    scratch = [
        vm((nz * pe, ub), BF), vm((SUP, ub, w), BF), vm((SUP, w, w), BF), vm((SUP + 1, dc, w), F32),
        vm((pe, w), BF), vm((SUP, ub), F32), vm((SUP, nz, pe, w), F32),
        vm((SUP, 2, hi, pe, w), BF), vm((SUP, 2, hi, pe, w), BF),
        vm((4, nx, ny * dc, 4 * pe), BF), vm((4, nx, ny * dc, 4 * pe), BF),
        vm((4, ny, 4 * dc, seg), BF), vm((4, 4 * dc, ub), BF),
        vm((4 * dc, w), BF), vm((nx, 4 * dc, w), BF),
        vm((SUP, 2 * dc, w // 2), BF), vm((nz, 2 * dc, w // 2), BF),
        vm((SUP, 2, 2 * dc, w // 2), BF), vm((nz, 2, 2 * dc, w // 2), BF),
        vm((tl, w), F32), vm((nx, ny * dc, tl), BF), vm((nx, ny * dc, tl), BF),
        vm((ny, dc, tl), F32), vm((ny, dc, tl), F32),
        vm((2 * dc, w // 2), BF), vm((2 * dc, w // 2), BF),
        vm((SUP, 2 * dc, w // 2), BF), vm((SUP, 2 * dc, w // 2), BF),
        vm((SUP, pe, w), BF), vm((SUP, dc, w), F32), vm((SUP, dc, w), F32),
        dma((13,)), dma((3,)), dma((SUP, 2, hi)), dma((SUP, 2, hi)),
        dma((4, nx)), dma((4, nx)), dma((4, ny)), dma((4, ny)),
        dma((ny,)), dma(()), dma((nx,)), dma((nx,)),
        dma((SUP,)), dma((nz,)), dma((SUP,)), dma((nz,)), dma((nx,)), dma((nx,)), dma((ny,)), dma((ny,)),
        dma((nz,)), dma((SUP,)), dma((nz,)), dma((SUP,)),
    ]
    cols, diag, sub = pl.pallas_call(
        functools.partial(kernel, nz, ny, nx),
        out_shape=(
            jax.ShapeDtypeStruct((SUP, pe, w), BF),
            jax.ShapeDtypeStruct((SUP, dc, w), F32),
            jax.ShapeDtypeStruct((SUP, dc, w), F32),
        ),
        in_specs=[any_spec] * 6 + [pl.BlockSpec(memory_space=pltpu.SMEM)],
        out_specs=(any_spec,) * 3,
        scratch_shapes=scratch,
        compiler_params=pltpu.CompilerParams(
            collective_id=0, has_side_effects=True, vmem_limit_bytes=64 * 1024 * 1024
        ),
        name="chain",
    )(g, m, chain_panel, diag_inverse, top, top_diag, pattern)
    return cols.reshape(SUP, 1, 1, pe, w), diag, sub


def solution(mesh):
    in_specs = (
        P(None, "rows", None, "cols"),
        P(None, "cols", None, None, None),
        P(),
        P(None, "rows", None),
        P("cols", "rows", None, None),
        P("rows", None),
        P(),
    )
    out_specs = (P(None, "cols", "rows", None, None), P(None, "rows", None), P(None, "rows", None))
    return jax.shard_map(local, mesh=mesh, in_specs=in_specs, out_specs=out_specs, check_vma=False)
```

```python
import functools

import jax
import jax.numpy as jnp
from jax import lax
from jax.experimental import pallas as pl
from jax.experimental.pallas import tpu as pltpu
from jax.sharding import PartitionSpec as P

BF = jnp.bfloat16
F32 = jnp.float32
MESH = pl.DeviceIdType.MESH
SUP = 4
OFF = {3: 0, 2: 0, 1: 0, 0: 0}


def mm(a, b):
    return jnp.dot(a, b, preferred_element_type=F32)


def mm_t(a, b):
    return lax.dot_general(a, b, (((1,), (1,)), ((), ())), preferred_element_type=F32)


def fold(x):
    half = x.shape[1] // 2
    return jnp.concatenate([x[:, :half], x[:, half:]], axis=0)


def unfold(x):
    rows = x.shape[0] // 2
    return jnp.concatenate([x[:rows], x[rows:]], axis=1)


def plane_w(k, nz):
    return (3 * k) % nz


def plane_s(k, nz):
    return (3 * k + 1) % nz


def tri(j, k):
    return j * (j + 1) // 2 + k


def kernel(nz, ny, nx, g_h, m_h, l_h, d_h, top_h, td_h, pat, cols_h, both_h,
           gv, mv, lv, dv, topv, mlv, pv, rss, rsr, xg, dg, ma, mat, accp, accs, cs, cr, ys, yr,
           fs, fr, fw, fv, gs, gw, ags, agw, nout, dout, sout,
           in_sem, out_sem, rs_ss, rs_rs, x_ss, x_rs, c_ss, c_rs, y_ss, y_rs,
           f_ss, f_rs, w_ss, w_rs, g_ss, g_rs, h_ss, h_rs):
    row = lax.axis_index("rows")
    c = lax.axis_index("cols")
    y = row // nx
    nc = nx // 2
    x = row % nx // 2
    co = row % 2
    pe = topv.shape[0]
    w = topv.shape[1]
    dc = w // (ny * nx)
    ku = nc * pe
    half = ny * dc

    def load(i, src, dst):
        return pltpu.make_async_copy(src, dst, in_sem.at[i])

    loads = {
        "g": load(0, g_h, gv), "top": load(2, top_h, topv),
        "d": load(3, d_h, dv.at[pl.ds(0, 4)]), "td": load(4, td_h, dv.at[4]),
    }
    for k in range(SUP):
        loads["m%d" % k] = load(5 + k, m_h.at[k], mv.at[k])
        loads["l%d" % k] = load(9 + k, l_h.at[k], lv.at[k])
    loads["g"].start()
    loads["m3"].start()

    def rcopy(src, dst, ss, rs, trow, tcol):
        return pltpu.make_async_remote_copy(src_ref=src, dst_ref=dst, send_sem=ss, recv_sem=rs,
                                            device_id=(trow, tcol), device_id_type=MESH)

    def xrow(p):
        return y * nx + (x + p) % nc * 2 + co

    def yrow(p):
        return (y + p) % ny * nx + x * 2 + co

    twin = y * nx + x * 2 + 1 - co

    bar = pltpu.get_barrier_semaphore()

    def sig(trow, tcol):
        pl.semaphore_signal(bar, inc=1, device_id=(trow, tcol), device_id_type=MESH)

    def over(n, f):
        def body(p, carry):
            f(p)
            return carry
        lax.fori_loop(1, n, body, 0)

    over(nc, lambda p: sig(xrow(p), c))
    sig(twin, c)
    over(ny, lambda p: sig(yrow(p), c))
    over(nz, lambda p: sig(row, (c + p) % nz))
    lane = lax.broadcasted_iota(jnp.int32, (1, 128), 1) // pe

    def mask_lanes(v, carry):
        for k in range(SUP):
            val = jnp.zeros((1, 128), F32)
            for q in range(128 // pe):
                one = pat[k, c * (ny * nx) + v * (128 // pe) + q].astype(F32)
                val = jnp.where(lane == q, one, val)
            mlv[pl.ds(k, 1), pl.ds(pl.multiple_of(v * 128, 128), 128)] = val
        return carry

    lax.fori_loop(0, ny * nx * pe // 128, mask_lanes, 0)
    loads["g"].wait()
    pl.semaphore_wait(bar, nc + (ny - 1) + (nz - 1))

    hi, lo = nz // 2, (nz - 1) // 2

    def hops(k, d):
        return lo + (k + d) % 2 if hi != lo else hi

    def rs_copy(k, d, s):
        to = (c + 1) % nz if d == 0 else (c + nz - 1) % nz
        return rcopy(rss.at[k, d, s], rsr.at[k, d, s], rs_ss.at[k, d, s], rs_rs.at[k, d, s], row, to)

    def rs_dest(k, d, s):
        h = hops(k, d) - s
        return (c + h) % nz if d == 0 else (c + nz - h) % nz

    def rs_step(k, d, s):
        val = pv[k, rs_dest(k, d, s)]
        if s > 0:
            rs_copy(k, d, s - 1).wait_recv()
            val = val + rsr[k, d, s - 1].astype(F32)
        rss[k, d, s] = val.astype(BF)
        rs_copy(k, d, s).start()

    def product_part(k):
        loads["m%d" % k].wait()
        for name in after[k]:
            loads[name].start()
        lhs = gv[...] * mlv[k:k + 1, :].astype(BF)
        pv[k] = mm(lhs, mv[k]).reshape(nz, pe, w)

    after = {3: ("m2", "top", "l3", "l2"), 2: ("m1", "l1", "l0"), 1: ("m0", "d", "td"), 0: ()}

    def x_copy(j, p):
        return rcopy(xg.at[j, x], xg.at[j, x], x_ss.at[j, p], x_rs.at[j, p], xrow(p), c)

    def x_wait(j, p):
        src = (x + nc - p) % nc
        rcopy(xg.at[j, src], xg.at[j, src], x_ss.at[j, p], x_rs.at[j, p], xrow(p), c).wait_recv()

    def d_copy(p):
        return rcopy(dg.at[x], dg.at[x], x_ss.at[5, p], x_rs.at[5, p], xrow(p), c)

    def d_wait(p):
        src = (x + nc - p) % nc
        rcopy(dg.at[src], dg.at[src], x_ss.at[5, p], x_rs.at[5, p], xrow(p), c).wait_recv()

    def x_send(j, val):
        xg[j, x] = val
        over(nc, lambda p: x_copy(j, p).start())

    def early_sends():
        for name in ("top", "d", "td"):
            loads[name].wait()
        x_send(4, topv[...])
        dg[x] = jnp.concatenate([dv[4], dv[3], dv[2], dv[1]], axis=0).astype(BF)
        over(nc, lambda p: d_copy(p).start())

    out_row = lax.broadcasted_iota(jnp.int32, (2 * half, w), 0)
    want = out_row // dc % ny * (nx * dc) + x * (2 * dc) + out_row // half * dc + out_row % dc
    pick = jnp.where(lax.broadcasted_iota(jnp.int32, (2 * half, w), 1) == want, 1.0, 0.0).astype(BF)

    def sel(v):
        return mm_t(pick, v).astype(BF)

    def panels():
        for name in ("l3", "l2", "l1", "l0"):
            loads[name].wait()
        for j in range(SUP):
            for q in range(nc):
                r = y * nx + q * 2 + co
                on = pat[j, c * (ny * nx) + r].astype(F32)
                rows = mv[j, pl.ds(pl.multiple_of(r * pe, pe), pe), :].astype(F32)
                ma[tri(j, j), q * pe:(q + 1) * pe] = (rows * on).astype(BF)
        for k in (2, 1, 0):
            stack = jnp.concatenate([ma[tri(j, k + 1)] for j in range(k + 1, SUP)], axis=0)
            res = mm(stack, lv[k]).astype(BF)
            for i, j in enumerate(range(k + 1, SUP)):
                ma[tri(j, k)] = res[ku * i:ku * (i + 1)]

    def panels_t():
        for j in range(SUP):
            for k in range(j + 1):
                mat[tri(j, k)] = sel(ma[tri(j, k)])

    def d_terms():
        over(nc, d_wait)
        nd = nc * dc
        mrow = lax.broadcasted_iota(jnp.int32, (nd, w), 0)
        at = y * (nx * dc) + mrow // dc * (2 * dc) + co * dc + mrow % dc
        one = jnp.where(lax.broadcasted_iota(jnp.int32, (nd, w), 1) == at, 1.0, 0.0).astype(BF)
        count = jnp.where(c == 0, 1.0, 0.0).astype(F32)
        right, left = [], []
        for k in (3, 2, 1, 0):
            mine = jnp.concatenate([dg[q, (3 - k) * dc:(4 - k) * dc] for q in range(nc)], axis=0)
            right, left = right + [mine], left + [one]
            res = mm(jnp.concatenate(right + left, axis=0), lv[k]).astype(BF)
            n = len(right)
            right = [res[nd * i:nd * (i + 1)] for i in range(n)]
            left = [res[nd * (n + i):nd * (n + i + 1)] for i in range(n)]
            accp[k] = count * mm(sel(res[nd * n:]), res[:nd * n])

    def event(j):
        over(nc, lambda p: x_wait(j, p))
        first_rows = xg[j].reshape(ku, w)
        cur = first_rows
        for k in range(j, -1, -1):
            if k < j:
                cur = mm(cur, lv[k]).astype(BF)
            if k < 4:
                add = None
                if j < 4:
                    add = -mm(mat[tri(j, k)], cur)
                if k < j:
                    more = mm(sel(cur), ma[tri(j - 1, k)])
                    add = more if add is None else add + more
                accp[k] += add
        if j > 0:
            accs[j - 1] = mm(sel(first_rows), ma[tri(j - 1, j - 1)])

    def span(j):
        return (1 if j == 4 else 0), (1 if j == 0 else 2)

    def mats(j):
        out = []
        if j < 4:
            out.append((0, accp.at[j]))
        if j > 0:
            out.append((1, accs.at[j - 1]))
        return out

    def c_copy(j):
        a, b = span(j)
        return rcopy(cs.at[j, a:b], cr.at[j, a:b], c_ss.at[j], c_rs.at[j], twin, c)

    def c_send(j):
        for i, ref in mats(j):
            cs[j, i] = ref[pl.ds(pl.multiple_of((1 - co) * half, half), half), :].astype(BF)
        c_copy(j).start()

    def y_copy(j, p):
        a, b = span(j)
        return rcopy(ys.at[j, (y + p) % ny, a:b], yr.at[j, y, a:b], y_ss.at[j, p], y_rs.at[j, p], yrow(p), c)

    def y_wait(j, p):
        a, b = span(j)
        src = (y + ny - p) % ny
        rcopy(ys.at[j, src, a:b], yr.at[j, src, a:b], y_ss.at[j, p], y_rs.at[j, p], yrow(p), c).wait_recv()

    def y_send(j):
        c_copy(j).wait_recv()
        for i, ref in mats(j):
            tot = ref[pl.ds(pl.multiple_of(co * half, half), half), :] + cr[j, i].astype(F32)
            tot = tot.reshape(ny, dc, w)
            tot = jnp.concatenate([tot[:, :, :w // 2], tot[:, :, w // 2:]], axis=1)
            ys[j, :, i] = tot.astype(BF)
        over(ny, lambda p: y_copy(j, p).start())
        for i, _ in mats(j):
            yr[j, y, i] = ys[j, y, i]

    def f_copy(k):
        return rcopy(fs.at[k], fr.at[c], f_ss.at[k], f_rs.at[c], row, plane_s(k, nz))

    def w_copy(k):
        return rcopy(fw.at[k], fv.at[c], w_ss.at[k], w_rs.at[c], row, plane_w(k, nz))

    def z_send(j):
        over(ny, lambda p: y_wait(j, p))
        for i, _ in mats(j):
            tot = yr[j, 0, i].astype(F32)
            for q in range(1, ny):
                tot = tot + yr[j, q, i].astype(F32)
            if i == 0:
                fw[j] = tot.astype(BF)
            else:
                fs[j - 1] = tot.astype(BF)
        if j < 4:
            @pl.when(c != plane_w(j, nz))
            def _():
                w_copy(j).start()

            @pl.when(c == plane_w(j, nz))
            def _():
                fv[c] = fw[j]
        if j > 0:
            @pl.when(c != plane_s(j - 1, nz))
            def _():
                f_copy(j - 1).start()

            @pl.when(c == plane_s(j - 1, nz))
            def _():
                fr[c] = fs[j - 1]

    def product(k):
        out = pv[k, c]
        for d in range(2):
            h = hops(k, d)
            if h > 0:
                rs_copy(k, d, h - 1).wait_recv()
                out = out + rsr[k, d, h - 1].astype(F32)
        return out

    def finish(k, carried):
        own_mask = pat[k, c * (ny * nx) + row].astype(F32)
        new = (-(product(k) + carried) * own_mask).astype(BF)
        nout[k] = new
        x_send(k, new)
        return new

    def carry():
        return mm(topv[...], lv[3])

    def early4():
        event(4)
        c_send(4)

    hooks = {0: [early_sends], 1: [panels], 2: [d_terms], 3: [early4], 4: [panels_t, lambda: y_send(4)], 5: []}
    state = {}
    for t in range(max(hi, 6)):
        for k in (3, 2, 1, 0):
            if t == OFF[k]:
                product_part(k)
                rs_step(k, 0, 0)
                rs_step(k, 1, 0)
        for k in (3, 2, 1, 0):
            s = t - OFF[k]
            for d in range(2):
                if 0 < s < hops(k, d):
                    rs_step(k, d, s)
        for f in hooks.get(t, ()):
            f()
    b43 = carry()
    z_send(4)
    n3 = finish(3, b43)
    n2 = finish(2, mm(n3, lv[2]))
    n1 = finish(1, mm(n2, lv[1]))
    finish(0, mm(n1, lv[0]))
    out_n = pltpu.make_async_copy(nout, cols_h, out_sem.at[0])
    out_n.start()
    event(3)
    c_send(3)
    event(2)
    c_send(2)
    y_send(3)
    event(1)
    c_send(1)
    y_send(2)
    event(0)
    c_send(0)
    y_send(1)
    y_send(0)
    for s in range(hi):
        for k in range(SUP):
            for d in range(2):
                if s < hops(k, d):
                    rs_copy(k, d, s).wait_send()
    z_send(3)
    z_send(2)
    z_send(1)
    z_send(0)

    def from_plane(p):
        return (c + nz - p) % nz

    def g_copy(k, p):
        return rcopy(gs, ags.at[k], g_ss.at[p], g_rs.at[k], row, (c + p) % nz)

    def h_copy(k, p):
        return rcopy(gw, agw.at[k], h_ss.at[p], h_rs.at[k], row, (c + p) % nz)

    for k in range(SUP):
        @pl.when(c == plane_s(k, nz))
        def _():
            def f_wait(p):
                src = from_plane(p)
                rcopy(fs.at[k], fr.at[src], f_ss.at[k], f_rs.at[src], row, src).wait_recv()

            over(nz, f_wait)
            gs[...] = jnp.sum(fr[...].astype(F32), axis=0).astype(BF)
            over(nz, lambda p: g_copy(k, p).start())
            ags[k] = gs[...]

    for k in range(SUP):
        @pl.when(c == plane_w(k, nz))
        def _():
            def w_wait(p):
                src = from_plane(p)
                rcopy(fw.at[k], fv.at[src], w_ss.at[k], w_rs.at[src], row, src).wait_recv()

            over(nz, w_wait)
            gw[...] = jnp.sum(fv[...].astype(F32), axis=0).astype(BF)
            over(nz, lambda p: h_copy(k, p).start())
            agw[k] = gw[...]

    def drain_x(p):
        for j in range(5):
            x_copy(j, p).wait_send()
        d_copy(p).wait_send()

    def drain_y(p):
        for j in range(5):
            y_copy(j, p).wait_send()

    over(nc, drain_x)
    over(ny, drain_y)
    for j in range(5):
        c_copy(j).wait_send()

    for k in range(SUP):
        @pl.when(c != plane_s(k, nz))
        def _():
            f_copy(k).wait_send()
            g_copy(k, 1).wait_recv()

        @pl.when(c != plane_w(k, nz))
        def _():
            w_copy(k).wait_send()

    for k in (3, 2, 1, 0):
        @pl.when(c != plane_w(k, nz))
        def _():
            h_copy(k, 1).wait_recv()

        dout[k] = dv[k] + unfold(agw[k].astype(F32))
    for k in range(SUP):
        prev = dout[k + 1] if k < 3 else dv[4]
        big = prev.astype(BF)
        small = (prev - big.astype(F32)).astype(BF)
        both = mm(jnp.concatenate([big, small], axis=0), lv[k])
        sout[k] = -(unfold(ags[k].astype(F32)) + both[:dc] + both[dc:])
    out_d = pltpu.make_async_copy(dout, both_h.at[pl.ds(0, SUP)], out_sem.at[1])
    out_s = pltpu.make_async_copy(sout, both_h.at[pl.ds(SUP, SUP)], out_sem.at[2])
    out_d.start()
    out_s.start()

    for k in range(SUP):
        @pl.when(c == plane_w(k, nz))
        def _():
            over(nz, lambda p: h_copy(k, p).wait_send())

    for k in range(SUP):
        @pl.when(c == plane_s(k, nz))
        def _():
            over(nz, lambda p: g_copy(k, p).wait_send())

    out_n.wait()
    out_d.wait()
    out_s.wait()


def local(known_inverse, lower_panel, chain_panel, diag_inverse, top_cols, top_diag, pattern):
    nr = lax.axis_size("rows")
    nz = lax.axis_size("cols")
    nx = 8 if nr >= 64 else 4
    ny = nr // nx
    pe = known_inverse.shape[2]
    w = lower_panel.shape[-1]
    dc = w // nr
    ub = nr * pe
    nc = nx // 2
    hi = nz // 2
    g = known_inverse.reshape(nz * pe, ub)
    m = lower_panel.reshape(SUP, ub, w)
    top = top_cols.reshape(pe, w)
    ku = nc * pe
    half = ny * dc
    dma = pltpu.SemaphoreType.DMA
    vm = pltpu.VMEM
    any_spec = pl.BlockSpec(memory_space=pltpu.HBM)
    scratch = [
        vm((nz * pe, ub), BF), vm((SUP, ub, w), BF), vm((SUP, w, w), BF), vm((SUP + 1, dc, w), F32),
        vm((pe, w), BF), vm((SUP, ub), F32), vm((SUP, nz, pe, w), F32),
        vm((SUP, 2, hi, pe, w), BF), vm((SUP, 2, hi, pe, w), BF),
        vm((5, nc, pe, w), BF), vm((nc, 4 * dc, w), BF), vm((10, ku, w), BF), vm((10, 2 * half, ku), BF),
        vm((SUP, 2 * half, w), F32), vm((SUP, 2 * half, w), F32),
        vm((5, 2, half, w), BF), vm((5, 2, half, w), BF),
        vm((5, ny, 2, 2 * dc, w // 2), BF), vm((5, ny, 2, 2 * dc, w // 2), BF),
        vm((SUP, 2 * dc, w // 2), BF), vm((nz, 2 * dc, w // 2), BF),
        vm((SUP, 2 * dc, w // 2), BF), vm((nz, 2 * dc, w // 2), BF),
        vm((2 * dc, w // 2), BF), vm((2 * dc, w // 2), BF),
        vm((SUP, 2 * dc, w // 2), BF), vm((SUP, 2 * dc, w // 2), BF),
        vm((SUP, pe, w), BF), vm((SUP, dc, w), F32), vm((SUP, dc, w), F32),
        dma((13,)), dma((3,)), dma((SUP, 2, hi)), dma((SUP, 2, hi)),
        dma((6, nc)), dma((6, nc)), dma((5,)), dma((5,)), dma((5, ny)), dma((5, ny)),
        dma((SUP,)), dma((nz,)), dma((SUP,)), dma((nz,)), dma((nz,)), dma((SUP,)), dma((nz,)), dma((SUP,)),
    ]
    cols, both = pl.pallas_call(
        functools.partial(kernel, nz, ny, nx),
        out_shape=(
            jax.ShapeDtypeStruct((SUP, pe, w), BF),
            jax.ShapeDtypeStruct((2 * SUP, dc, w), F32),
        ),
        in_specs=[any_spec] * 6 + [pl.BlockSpec(memory_space=pltpu.SMEM)],
        out_specs=(any_spec,) * 2,
        scratch_shapes=scratch,
        compiler_params=pltpu.CompilerParams(
            collective_id=0, has_side_effects=True, vmem_limit_bytes=64 * 1024 * 1024
        ),
        name="chain",
    )(g, m, chain_panel, diag_inverse, top, top_diag, pattern)
    diag, sub = both[:SUP], both[SUP:]
    return cols.reshape(SUP, 1, 1, pe, w), diag, sub


def solution(mesh):
    in_specs = (
        P(None, "rows", None, "cols"),
        P(None, "cols", None, None, None),
        P(),
        P(None, "rows", None),
        P("cols", "rows", None, None),
        P("rows", None),
        P(),
    )
    out_specs = (P(None, "cols", "rows", None, None), P(None, "rows", None), P(None, "rows", None))
    return jax.shard_map(local, mesh=mesh, in_specs=in_specs, out_specs=out_specs, check_vma=False)
```

```python
import functools

import jax
import jax.numpy as jnp
from jax import lax
from jax.experimental import pallas as pl
from jax.experimental.pallas import tpu as pltpu
from jax.sharding import PartitionSpec as P

BF = jnp.bfloat16
F32 = jnp.float32
MESH = pl.DeviceIdType.MESH
SUP = 4
OFF = {3: 0, 2: 0, 1: 1, 0: 1}


def mm(a, b):
    return jnp.dot(a, b, preferred_element_type=F32)


def mm_t(a, b):
    return lax.dot_general(a, b, (((1,), (1,)), ((), ())), preferred_element_type=F32)


def fold(x):
    half = x.shape[1] // 2
    return jnp.concatenate([x[:, :half], x[:, half:]], axis=0)


def unfold(x):
    rows = x.shape[0] // 2
    return jnp.concatenate([x[:rows], x[rows:]], axis=1)


def plane_w(k, nz):
    return (3 * k) % nz


def plane_s(k, nz):
    return (3 * k + 1) % nz


def tri(j, k):
    return j * (j + 1) // 2 + k


def kernel(nz, ny, nx, g_h, m_h, l_h, d_h, top_h, td_h, pat, cols_h, diag_h, sub_h,
           gv, mv, lv, dv, topv, mlv, pv, rss, rsr, xg, dg, ma, mat, accp, accs, cs, cr, ys, yr,
           fs, fr, fw, fv, gs, gw, ags, agw, nout, dout, sout,
           in_sem, out_sem, rs_ss, rs_rs, x_ss, x_rs, c_ss, c_rs, y_ss, y_rs,
           f_ss, f_rs, w_ss, w_rs, g_ss, g_rs, h_ss, h_rs):
    row = lax.axis_index("rows")
    c = lax.axis_index("cols")
    y = row // nx
    nc = nx // 2
    x = row % nx // 2
    co = row % 2
    pe = topv.shape[0]
    w = topv.shape[1]
    dc = w // (ny * nx)
    ku = nc * pe
    half = ny * dc

    def load(i, src, dst):
        return pltpu.make_async_copy(src, dst, in_sem.at[i])

    loads = {
        "g": load(0, g_h, gv), "top": load(2, top_h, topv),
        "d": load(3, d_h, dv.at[pl.ds(0, 4)]), "td": load(4, td_h, dv.at[4]),
    }
    for k in range(SUP):
        loads["m%d" % k] = load(5 + k, m_h.at[k], mv.at[k])
        loads["l%d" % k] = load(9 + k, l_h.at[k], lv.at[k])
    loads["g"].start()
    loads["m3"].start()
    loads["m2"].start()

    def rcopy(src, dst, ss, rs, trow, tcol):
        return pltpu.make_async_remote_copy(src_ref=src, dst_ref=dst, send_sem=ss, recv_sem=rs,
                                            device_id=(trow, tcol), device_id_type=MESH)

    def xrow(p):
        return y * nx + (x + p) % nc * 2 + co

    def yrow(p):
        return (y + p) % ny * nx + x * 2 + co

    twin = y * nx + x * 2 + 1 - co

    bar = pltpu.get_barrier_semaphore()

    def sig(trow, tcol):
        pl.semaphore_signal(bar, inc=1, device_id=(trow, tcol), device_id_type=MESH)

    def over(n, f):
        def body(p, carry):
            f(p)
            return carry
        lax.fori_loop(1, n, body, 0)

    over(nc, lambda p: sig(xrow(p), c))
    sig(twin, c)
    over(ny, lambda p: sig(yrow(p), c))
    over(nz, lambda p: sig(row, (c + p) % nz))
    lane = lax.broadcasted_iota(jnp.int32, (1, 128), 1) // pe

    def mask_lanes(v, carry):
        for k in range(SUP):
            val = jnp.zeros((1, 128), F32)
            for q in range(128 // pe):
                one = pat[k, c * (ny * nx) + v * (128 // pe) + q].astype(F32)
                val = jnp.where(lane == q, one, val)
            mlv[pl.ds(k, 1), pl.ds(pl.multiple_of(v * 128, 128), 128)] = val
        return carry

    lax.fori_loop(0, ny * nx * pe // 128, mask_lanes, 0)
    loads["g"].wait()

    hi, lo = nz // 2, (nz - 1) // 2

    def hops(k, d):
        return lo + (k + d) % 2 if hi != lo else hi

    def rs_copy(k, d, s):
        to = (c + 1) % nz if d == 0 else (c + nz - 1) % nz
        return rcopy(rss.at[k, d, s], rsr.at[k, d, s], rs_ss.at[k, d, s], rs_rs.at[k, d, s], row, to)

    def rs_dest(k, d, s):
        h = hops(k, d) - s
        return (c + h) % nz if d == 0 else (c + nz - h) % nz

    def rs_step(k, d, s):
        val = pv[k, rs_dest(k, d, s)]
        if s > 0:
            rs_copy(k, d, s - 1).wait_recv()
            val = val + rsr[k, d, s - 1].astype(F32)
        rss[k, d, s] = val.astype(BF)
        rs_copy(k, d, s).start()

    def product_part(k):
        loads["m%d" % k].wait()
        for name in after[k]:
            loads[name].start()
        lhs = gv[...] * mlv[k:k + 1, :].astype(BF)
        pv[k] = mm(lhs, mv[k]).reshape(nz, pe, w)

    after = {3: ("m1",), 2: ("m0", "top", "d", "td", "l3", "l2", "l1", "l0"), 1: (), 0: ()}

    def x_copy(j, p):
        return rcopy(xg.at[j, x], xg.at[j, x], x_ss.at[j, p], x_rs.at[j, p], xrow(p), c)

    def x_wait(j, p):
        src = (x + nc - p) % nc
        rcopy(xg.at[j, src], xg.at[j, src], x_ss.at[j, p], x_rs.at[j, p], xrow(p), c).wait_recv()

    def d_copy(p):
        return rcopy(dg.at[x], dg.at[x], x_ss.at[5, p], x_rs.at[5, p], xrow(p), c)

    def d_wait(p):
        src = (x + nc - p) % nc
        rcopy(dg.at[src], dg.at[src], x_ss.at[5, p], x_rs.at[5, p], xrow(p), c).wait_recv()

    def x_send(j, val):
        xg[j, x] = val
        over(nc, lambda p: x_copy(j, p).start())

    def early_sends():
        for name in ("top", "d", "td"):
            loads[name].wait()
        x_send(4, topv[...])
        dg[x] = jnp.concatenate([dv[4], dv[3], dv[2], dv[1]], axis=0).astype(BF)
        over(nc, lambda p: d_copy(p).start())

    out_row = lax.broadcasted_iota(jnp.int32, (2 * half, w), 0)
    want = out_row // dc % ny * (nx * dc) + x * (2 * dc) + out_row // half * dc + out_row % dc
    pick = jnp.where(lax.broadcasted_iota(jnp.int32, (2 * half, w), 1) == want, 1.0, 0.0).astype(BF)

    def sel(v):
        return mm_t(pick, v).astype(BF)

    def panels():
        for name in ("l3", "l2", "l1", "l0"):
            loads[name].wait()
        for j in range(SUP):
            for q in range(nc):
                r = y * nx + q * 2 + co
                on = pat[j, c * (ny * nx) + r].astype(F32)
                rows = mv[j, pl.ds(pl.multiple_of(r * pe, pe), pe), :].astype(F32)
                ma[tri(j, j), q * pe:(q + 1) * pe] = (rows * on).astype(BF)
        for k in (2, 1, 0):
            stack = jnp.concatenate([ma[tri(j, k + 1)] for j in range(k + 1, SUP)], axis=0)
            res = mm(stack, lv[k]).astype(BF)
            for i, j in enumerate(range(k + 1, SUP)):
                ma[tri(j, k)] = res[ku * i:ku * (i + 1)]

    def panels_t():
        for j in range(SUP):
            for k in range(j + 1):
                mat[tri(j, k)] = sel(ma[tri(j, k)])

    def d_terms():
        over(nc, d_wait)
        nd = nc * dc
        mrow = lax.broadcasted_iota(jnp.int32, (nd, w), 0)
        at = y * (nx * dc) + mrow // dc * (2 * dc) + co * dc + mrow % dc
        one = jnp.where(lax.broadcasted_iota(jnp.int32, (nd, w), 1) == at, 1.0, 0.0).astype(BF)
        count = jnp.where(c == 0, 1.0, 0.0).astype(F32)
        right, left = [], []
        for k in (3, 2, 1, 0):
            mine = jnp.concatenate([dg[q, (3 - k) * dc:(4 - k) * dc] for q in range(nc)], axis=0)
            right, left = right + [mine], left + [one]
            res = mm(jnp.concatenate(right + left, axis=0), lv[k]).astype(BF)
            n = len(right)
            right = [res[nd * i:nd * (i + 1)] for i in range(n)]
            left = [res[nd * (n + i):nd * (n + i + 1)] for i in range(n)]
            accp[k] = count * mm(sel(res[nd * n:]), res[:nd * n])

    def event(j):
        over(nc, lambda p: x_wait(j, p))
        first_rows = xg[j].reshape(ku, w)
        cur = first_rows
        for k in range(j, -1, -1):
            if k < j:
                cur = mm(cur, lv[k]).astype(BF)
            if k < 4:
                add = None
                if j < 4:
                    add = -mm(mat[tri(j, k)], cur)
                if k < j:
                    more = mm(sel(cur), ma[tri(j - 1, k)])
                    add = more if add is None else add + more
                accp[k] += add
        if j > 0:
            accs[j - 1] = mm(sel(first_rows), ma[tri(j - 1, j - 1)])

    def span(j):
        return (1 if j == 4 else 0), (1 if j == 0 else 2)

    def mats(j):
        out = []
        if j < 4:
            out.append((0, accp.at[j]))
        if j > 0:
            out.append((1, accs.at[j - 1]))
        return out

    def c_copy(j):
        a, b = span(j)
        return rcopy(cs.at[j, a:b], cr.at[j, a:b], c_ss.at[j], c_rs.at[j], twin, c)

    def c_send(j):
        for i, ref in mats(j):
            cs[j, i] = ref[pl.ds(pl.multiple_of((1 - co) * half, half), half), :].astype(BF)
        c_copy(j).start()

    def y_copy(j, p):
        a, b = span(j)
        return rcopy(ys.at[j, (y + p) % ny, a:b], yr.at[j, y, a:b], y_ss.at[j, p], y_rs.at[j, p], yrow(p), c)

    def y_wait(j, p):
        a, b = span(j)
        src = (y + ny - p) % ny
        rcopy(ys.at[j, src, a:b], yr.at[j, src, a:b], y_ss.at[j, p], y_rs.at[j, p], yrow(p), c).wait_recv()

    def y_send(j):
        c_copy(j).wait_recv()
        for i, ref in mats(j):
            tot = ref[pl.ds(pl.multiple_of(co * half, half), half), :] + cr[j, i].astype(F32)
            tot = tot.reshape(ny, dc, w)
            tot = jnp.concatenate([tot[:, :, :w // 2], tot[:, :, w // 2:]], axis=1)
            ys[j, :, i] = tot.astype(BF)
        over(ny, lambda p: y_copy(j, p).start())
        for i, _ in mats(j):
            yr[j, y, i] = ys[j, y, i]

    def f_copy(k):
        return rcopy(fs.at[k], fr.at[c], f_ss.at[k], f_rs.at[c], row, plane_s(k, nz))

    def w_copy(k):
        return rcopy(fw.at[k], fv.at[c], w_ss.at[k], w_rs.at[c], row, plane_w(k, nz))

    def z_send(j):
        over(ny, lambda p: y_wait(j, p))
        for i, _ in mats(j):
            tot = yr[j, 0, i].astype(F32)
            for q in range(1, ny):
                tot = tot + yr[j, q, i].astype(F32)
            if i == 0:
                fw[j] = tot.astype(BF)
            else:
                fs[j - 1] = tot.astype(BF)
        if j < 4:
            @pl.when(c != plane_w(j, nz))
            def _():
                w_copy(j).start()

            @pl.when(c == plane_w(j, nz))
            def _():
                fv[c] = fw[j]
        if j > 0:
            @pl.when(c != plane_s(j - 1, nz))
            def _():
                f_copy(j - 1).start()

            @pl.when(c == plane_s(j - 1, nz))
            def _():
                fr[c] = fs[j - 1]

    def product(k):
        out = pv[k, c]
        for d in range(2):
            h = hops(k, d)
            if h > 0:
                rs_copy(k, d, h - 1).wait_recv()
                out = out + rsr[k, d, h - 1].astype(F32)
        return out

    def finish(k, carried):
        own_mask = pat[k, c * (ny * nx) + row].astype(F32)
        new = (-(product(k) + carried) * own_mask).astype(BF)
        nout[k] = new
        x_send(k, new)
        return new

    def early4():
        event(4)
        c_send(4)

    chain = {}

    def upper():
        chain[3] = finish(3, mm(topv[...], lv[3]))
        chain[2] = finish(2, mm(chain[3], lv[2]))
        z_send(4)

    hooks = {1: [early_sends], 2: [panels], 3: [d_terms], 4: [early4], 5: [panels_t, lambda: y_send(4)], 6: [upper]}
    for t in range(max(hi + 1, 7)):
        fresh = [k for k in (3, 2, 1, 0) if t == OFF[k]]
        if t == 0:
            for k in fresh:
                product_part(k)
            pl.semaphore_wait(bar, nc + (ny - 1) + (nz - 1))
        for k in fresh:
            if t > 0:
                product_part(k)
            rs_step(k, 0, 0)
            rs_step(k, 1, 0)
        for k in (3, 2, 1, 0):
            s = t - OFF[k]
            for d in range(2):
                if 0 < s < hops(k, d):
                    rs_step(k, d, s)
        for f in hooks.get(t, ()):
            f()
    n1 = finish(1, mm(chain[2], lv[1]))
    finish(0, mm(n1, lv[0]))
    out_n = pltpu.make_async_copy(nout, cols_h, out_sem.at[0])
    out_n.start()
    event(3)
    c_send(3)
    event(2)
    c_send(2)
    y_send(3)
    event(1)
    c_send(1)
    y_send(2)
    event(0)
    c_send(0)
    y_send(1)
    y_send(0)
    for s in range(hi):
        for k in range(SUP):
            for d in range(2):
                if s < hops(k, d):
                    rs_copy(k, d, s).wait_send()
    z_send(3)
    z_send(2)
    z_send(1)
    z_send(0)

    def from_plane(p):
        return (c + nz - p) % nz

    def g_copy(k, p):
        return rcopy(gs, ags.at[k], g_ss.at[p], g_rs.at[k], row, (c + p) % nz)

    def h_copy(k, p):
        return rcopy(gw, agw.at[k], h_ss.at[p], h_rs.at[k], row, (c + p) % nz)

    for k in range(SUP):
        @pl.when(c == plane_s(k, nz))
        def _():
            def f_wait(p):
                src = from_plane(p)
                rcopy(fs.at[k], fr.at[src], f_ss.at[k], f_rs.at[src], row, src).wait_recv()

            over(nz, f_wait)
            gs[...] = jnp.sum(fr[...].astype(F32), axis=0).astype(BF)
            over(nz, lambda p: g_copy(k, p).start())
            ags[k] = gs[...]

    for k in range(SUP):
        @pl.when(c == plane_w(k, nz))
        def _():
            def w_wait(p):
                src = from_plane(p)
                rcopy(fw.at[k], fv.at[src], w_ss.at[k], w_rs.at[src], row, src).wait_recv()

            over(nz, w_wait)
            gw[...] = jnp.sum(fv[...].astype(F32), axis=0).astype(BF)
            over(nz, lambda p: h_copy(k, p).start())
            agw[k] = gw[...]

    def drain_x(p):
        for j in range(5):
            x_copy(j, p).wait_send()
        d_copy(p).wait_send()

    def drain_y(p):
        for j in range(5):
            y_copy(j, p).wait_send()

    over(nc, drain_x)
    over(ny, drain_y)
    for j in range(5):
        c_copy(j).wait_send()

    for k in range(SUP):
        @pl.when(c != plane_s(k, nz))
        def _():
            f_copy(k).wait_send()
            g_copy(k, 1).wait_recv()

        @pl.when(c != plane_w(k, nz))
        def _():
            w_copy(k).wait_send()

    def take_p(k):
        @pl.when(c != plane_w(k, nz))
        def _():
            h_copy(k, 1).wait_recv()

        dout[k] = dv[k] + unfold(agw[k].astype(F32))

    for k in (3, 2, 1, 0):
        if k < 3:
            take_p(k + 1)
        prev = dout[k + 1] if k < 3 else dv[4]
        big = prev.astype(BF)
        small = (prev - big.astype(F32)).astype(BF)
        both = mm(jnp.concatenate([big, small], axis=0), lv[k])
        sout[k] = -(unfold(ags[k].astype(F32)) + both[:dc] + both[dc:])
    out_s = pltpu.make_async_copy(sout, sub_h, out_sem.at[2])
    out_d = pltpu.make_async_copy(dout.at[1:SUP], diag_h.at[1:SUP], out_sem.at[1])
    out_s.start()
    out_d.start()
    take_p(0)
    out_z = pltpu.make_async_copy(dout.at[0], diag_h.at[0], out_sem.at[3])
    out_z.start()

    for k in range(SUP):
        @pl.when(c == plane_w(k, nz))
        def _():
            over(nz, lambda p: h_copy(k, p).wait_send())

    for k in range(SUP):
        @pl.when(c == plane_s(k, nz))
        def _():
            over(nz, lambda p: g_copy(k, p).wait_send())

    out_n.wait()
    out_d.wait()
    out_s.wait()
    out_z.wait()


def hand_over(a, b, d, a_out, b_out, d_out, a_v, b_v, d_v, sem, sem_out):
    trips = ((a, a_v, a_out), (b, b_v, b_out), (d, d_v, d_out))
    loads = [pltpu.make_async_copy(src, mid, sem.at[i]) for i, (src, mid, _) in enumerate(trips)]
    stores = [pltpu.make_async_copy(mid, dst, sem_out.at[i]) for i, (_, mid, dst) in enumerate(trips)]
    for load in loads:
        load.start()
    for load, store in zip(loads, stores):
        load.wait()
        store.start()
    for store in stores:
        store.wait()


def local(known_inverse, lower_panel, chain_panel, diag_inverse, top_cols, top_diag, pattern):
    nr = lax.axis_size("rows")
    nz = lax.axis_size("cols")
    nx = 8 if nr >= 64 else 4
    ny = nr // nx
    pe = known_inverse.shape[2]
    w = lower_panel.shape[-1]
    dc = w // nr
    ub = nr * pe
    nc = nx // 2
    hi = nz // 2
    g = known_inverse.reshape(nz * pe, ub)
    m = lower_panel.reshape(SUP, ub, w)
    top = top_cols.reshape(pe, w)
    ku = nc * pe
    half = ny * dc
    dma = pltpu.SemaphoreType.DMA
    vm = pltpu.VMEM
    any_spec = pl.BlockSpec(memory_space=pltpu.HBM)
    scratch = [
        vm((nz * pe, ub), BF), vm((SUP, ub, w), BF), vm((SUP, w, w), BF), vm((SUP + 1, dc, w), F32),
        vm((pe, w), BF), vm((SUP, ub), F32), vm((SUP, nz, pe, w), F32),
        vm((SUP, 2, hi, pe, w), BF), vm((SUP, 2, hi, pe, w), BF),
        vm((5, nc, pe, w), BF), vm((nc, 4 * dc, w), BF), vm((10, ku, w), BF), vm((10, 2 * half, ku), BF),
        vm((SUP, 2 * half, w), F32), vm((SUP, 2 * half, w), F32),
        vm((5, 2, half, w), BF), vm((5, 2, half, w), BF),
        vm((5, ny, 2, 2 * dc, w // 2), BF), vm((5, ny, 2, 2 * dc, w // 2), BF),
        vm((SUP, 2 * dc, w // 2), BF), vm((nz, 2 * dc, w // 2), BF),
        vm((SUP, 2 * dc, w // 2), BF), vm((nz, 2 * dc, w // 2), BF),
        vm((2 * dc, w // 2), BF), vm((2 * dc, w // 2), BF),
        vm((SUP, 2 * dc, w // 2), BF), vm((SUP, 2 * dc, w // 2), BF),
        vm((SUP, pe, w), BF), vm((SUP, dc, w), F32), vm((SUP, dc, w), F32),
        dma((13,)), dma((4,)), dma((SUP, 2, hi)), dma((SUP, 2, hi)),
        dma((6, nc)), dma((6, nc)), dma((5,)), dma((5,)), dma((5, ny)), dma((5, ny)),
        dma((SUP,)), dma((nz,)), dma((SUP,)), dma((nz,)), dma((nz,)), dma((SUP,)), dma((nz,)), dma((SUP,)),
    ]
    outs = pl.pallas_call(
        functools.partial(kernel, nz, ny, nx),
        out_shape=(
            jax.ShapeDtypeStruct((SUP, pe, w), BF),
            jax.ShapeDtypeStruct((SUP, dc, w), F32),
            jax.ShapeDtypeStruct((SUP, dc, w), F32),
        ),
        in_specs=[any_spec] * 6 + [pl.BlockSpec(memory_space=pltpu.SMEM)],
        out_specs=(any_spec,) * 3,
        scratch_shapes=scratch,
        compiler_params=pltpu.CompilerParams(
            collective_id=0, has_side_effects=True, vmem_limit_bytes=64 * 1024 * 1024
        ),
        name="chain",
    )(g, m, chain_panel, diag_inverse, top, top_diag, pattern)
    cols, diag, sub = pl.pallas_call(
        hand_over,
        out_shape=tuple(jax.ShapeDtypeStruct(o.shape, o.dtype) for o in outs),
        in_specs=[any_spec] * 3,
        out_specs=(any_spec,) * 3,
        scratch_shapes=[vm(o.shape, o.dtype) for o in outs] + [dma((3,)), dma((3,))],
        name="hand_over",
    )(*outs)
    return cols.reshape(SUP, 1, 1, pe, w), diag, sub


def solution(mesh):
    in_specs = (
        P(None, "rows", None, "cols"),
        P(None, "cols", None, None, None),
        P(),
        P(None, "rows", None),
        P("cols", "rows", None, None),
        P("rows", None),
        P(),
    )
    out_specs = (P(None, "cols", "rows", None, None), P(None, "rows", None), P(None, "rows", None))
    return jax.shard_map(local, mesh=mesh, in_specs=in_specs, out_specs=out_specs, check_vma=False)
```

```python
import functools

import jax
import jax.numpy as jnp
from jax import lax
from jax.experimental import pallas as pl
from jax.experimental.pallas import tpu as pltpu
from jax.sharding import PartitionSpec as P

BF = jnp.bfloat16
F32 = jnp.float32
MESH = pl.DeviceIdType.MESH
SUP = 4
OFF = {3: 0, 2: 0, 1: 0, 0: 0}


def mm(a, b):
    return jnp.dot(a, b, preferred_element_type=F32)


def mm_t(a, b):
    return lax.dot_general(a, b, (((1,), (1,)), ((), ())), preferred_element_type=F32)


def fold(x):
    half = x.shape[1] // 2
    return jnp.concatenate([x[:, :half], x[:, half:]], axis=0)


def unfold(x):
    rows = x.shape[0] // 2
    return jnp.concatenate([x[:rows], x[rows:]], axis=1)


def plane_w(k, nz):
    return (3 * k) % nz


def plane_s(k, nz):
    return (3 * k + 1) % nz


def tri(j, k):
    return j * (j + 1) // 2 + k


def kernel(nz, ny, nx, g_h, m_h, l_h, d_h, top_h, td_h, pat, cols_h, diag_h, sub_h,
           gv, mv, lv, dv, topv, mlv, pv, rss, rsr, xg, dg, ma, mat, accp, accs, cs, cr, ys, yr,
           fs, fr, fw, fv, gs, gw, ags, agw, nout, dout, sout,
           in_sem, out_sem, rs_ss, rs_rs, x_ss, x_rs, c_ss, c_rs, y_ss, y_rs,
           f_ss, f_rs, w_ss, w_rs, g_ss, g_rs, h_ss, h_rs):
    row = lax.axis_index("rows")
    c = lax.axis_index("cols")
    y = row // nx
    nc = nx // 2
    x = row % nx // 2
    co = row % 2
    pe = topv.shape[0]
    w = topv.shape[1]
    dc = w // (ny * nx)
    ku = nc * pe
    half = ny * dc

    def load(i, src, dst):
        return pltpu.make_async_copy(src, dst, in_sem.at[i])

    loads = {
        "g": load(0, g_h, gv), "top": load(2, top_h, topv),
        "d": load(3, d_h, dv.at[pl.ds(0, 4)]), "td": load(4, td_h, dv.at[4]),
    }
    for k in range(SUP):
        loads["m%d" % k] = load(5 + k, m_h.at[k], mv.at[k])
        loads["l%d" % k] = load(9 + k, l_h.at[k], lv.at[k])
    loads["g"].start()
    loads["m3"].start()
    loads["m2"].start()

    def rcopy(src, dst, ss, rs, trow, tcol):
        return pltpu.make_async_remote_copy(src_ref=src, dst_ref=dst, send_sem=ss, recv_sem=rs,
                                            device_id=(trow, tcol), device_id_type=MESH)

    def xrow(p):
        return y * nx + (x + p) % nc * 2 + co

    def yrow(p):
        return (y + p) % ny * nx + x * 2 + co

    twin = y * nx + x * 2 + 1 - co

    bar = pltpu.get_barrier_semaphore()

    def sig(trow, tcol):
        pl.semaphore_signal(bar, inc=1, device_id=(trow, tcol), device_id_type=MESH)

    def over(n, f):
        for p in sorted(range(1, n), key=lambda p: -min(p, n - p)):
            f(p)

    over(nc, lambda p: sig(xrow(p), c))
    sig(twin, c)
    over(ny, lambda p: sig(yrow(p), c))
    over(nz, lambda p: sig(row, (c + p) % nz))
    lane = lax.broadcasted_iota(jnp.int32, (1, 128), 1) // pe

    def mask_lanes(v, carry):
        for k in range(SUP):
            val = jnp.zeros((1, 128), F32)
            for q in range(128 // pe):
                one = pat[k, c * (ny * nx) + v * (128 // pe) + q].astype(F32)
                val = jnp.where(lane == q, one, val)
            mlv[pl.ds(k, 1), pl.ds(pl.multiple_of(v * 128, 128), 128)] = val
        return carry

    lax.fori_loop(0, ny * nx * pe // 128, mask_lanes, 0)
    loads["g"].wait()

    hi, lo = nz // 2, (nz - 1) // 2

    def hops(k, d):
        return lo + (k + d) % 2 if hi != lo else hi

    def rs_copy(k, d, s):
        to = (c + 1) % nz if d == 0 else (c + nz - 1) % nz
        return rcopy(rss.at[k, d, s], rsr.at[k, d, s], rs_ss.at[k, d, s], rs_rs.at[k, d, s], row, to)

    def rs_dest(k, d, s):
        h = hops(k, d) - s
        return (c + h) % nz if d == 0 else (c + nz - h) % nz

    def rs_step(k, d, s):
        val = pv[k, rs_dest(k, d, s)]
        if s > 0:
            rs_copy(k, d, s - 1).wait_recv()
            val = val + rsr[k, d, s - 1].astype(F32)
        rss[k, d, s] = val.astype(BF)
        rs_copy(k, d, s).start()

    def product_part(k):
        loads["m%d" % k].wait()
        for name in after[k]:
            loads[name].start()
        lhs = gv[...] * mlv[k:k + 1, :].astype(BF)
        pv[k] = mm(lhs, mv[k]).reshape(nz, pe, w)

    after = {3: ("m1",), 2: ("m0", "top", "d", "td", "l3", "l2", "l1", "l0"), 1: (), 0: ()}

    def x_copy(j, p):
        return rcopy(xg.at[j, x], xg.at[j, x], x_ss.at[j, p], x_rs.at[j, p], xrow(p), c)

    def x_wait(j, p):
        src = (x + nc - p) % nc
        rcopy(xg.at[j, src], xg.at[j, src], x_ss.at[j, p], x_rs.at[j, p], xrow(p), c).wait_recv()

    def d_copy(p):
        return rcopy(dg.at[x], dg.at[x], x_ss.at[5, p], x_rs.at[5, p], xrow(p), c)

    def d_wait(p):
        src = (x + nc - p) % nc
        rcopy(dg.at[src], dg.at[src], x_ss.at[5, p], x_rs.at[5, p], xrow(p), c).wait_recv()

    def x_send(j, val):
        xg[j, x] = val
        over(nc, lambda p: x_copy(j, p).start())

    def early_sends():
        for name in ("top", "d", "td"):
            loads[name].wait()
        x_send(4, topv[...])
        dg[x] = jnp.concatenate([dv[4], dv[3], dv[2], dv[1]], axis=0).astype(BF)
        over(nc, lambda p: d_copy(p).start())

    out_row = lax.broadcasted_iota(jnp.int32, (2 * half, w), 0)
    want = out_row // dc % ny * (nx * dc) + x * (2 * dc) + out_row // half * dc + out_row % dc
    pick = jnp.where(lax.broadcasted_iota(jnp.int32, (2 * half, w), 1) == want, 1.0, 0.0).astype(BF)

    def sel(v):
        return mm_t(pick, v).astype(BF)

    def panels():
        for name in ("l3", "l2", "l1", "l0"):
            loads[name].wait()
        for j in range(SUP):
            for q in range(nc):
                r = y * nx + q * 2 + co
                on = pat[j, c * (ny * nx) + r].astype(F32)
                rows = mv[j, pl.ds(pl.multiple_of(r * pe, pe), pe), :].astype(F32)
                ma[tri(j, j), q * pe:(q + 1) * pe] = (rows * on).astype(BF)
        for k in (2, 1, 0):
            stack = jnp.concatenate([ma[tri(j, k + 1)] for j in range(k + 1, SUP)], axis=0)
            res = mm(stack, lv[k]).astype(BF)
            for i, j in enumerate(range(k + 1, SUP)):
                ma[tri(j, k)] = res[ku * i:ku * (i + 1)]

    def panels_t():
        for j in range(SUP):
            for k in range(j + 1):
                mat[tri(j, k)] = sel(ma[tri(j, k)])

    def d_terms():
        over(nc, d_wait)
        nd = nc * dc
        mrow = lax.broadcasted_iota(jnp.int32, (nd, w), 0)
        at = y * (nx * dc) + mrow // dc * (2 * dc) + co * dc + mrow % dc
        one = jnp.where(lax.broadcasted_iota(jnp.int32, (nd, w), 1) == at, 1.0, 0.0).astype(BF)
        count = jnp.where(c == 0, 1.0, 0.0).astype(F32)
        right, left = [], []
        for k in (3, 2, 1, 0):
            mine = jnp.concatenate([dg[q, (3 - k) * dc:(4 - k) * dc] for q in range(nc)], axis=0)
            right, left = right + [mine], left + [one]
            res = mm(jnp.concatenate(right + left, axis=0), lv[k]).astype(BF)
            n = len(right)
            right = [res[nd * i:nd * (i + 1)] for i in range(n)]
            left = [res[nd * (n + i):nd * (n + i + 1)] for i in range(n)]
            accp[k] = count * mm(sel(res[nd * n:]), res[:nd * n])

    def event(j):
        over(nc, lambda p: x_wait(j, p))
        first_rows = xg[j].reshape(ku, w)
        cur = first_rows
        for k in range(j, -1, -1):
            if k < j:
                cur = mm(cur, lv[k]).astype(BF)
            if k < 4:
                add = None
                if j < 4:
                    add = -mm(mat[tri(j, k)], cur)
                if k < j:
                    more = mm(sel(cur), ma[tri(j - 1, k)])
                    add = more if add is None else add + more
                accp[k] += add
        if j > 0:
            accs[j - 1] = mm(sel(first_rows), ma[tri(j - 1, j - 1)])

    def span(j):
        return (1 if j == 4 else 0), (1 if j == 0 else 2)

    def mats(j):
        out = []
        if j < 4:
            out.append((0, accp.at[j]))
        if j > 0:
            out.append((1, accs.at[j - 1]))
        return out

    def c_copy(j):
        a, b = span(j)
        return rcopy(cs.at[j, a:b], cr.at[j, a:b], c_ss.at[j], c_rs.at[j], twin, c)

    def c_send(j):
        for i, ref in mats(j):
            cs[j, i] = ref[pl.ds(pl.multiple_of((1 - co) * half, half), half), :].astype(BF)
        c_copy(j).start()

    def y_copy(j, p):
        a, b = span(j)
        return rcopy(ys.at[j, (y + p) % ny, a:b], yr.at[j, y, a:b], y_ss.at[j, p], y_rs.at[j, p], yrow(p), c)

    def y_wait(j, p):
        a, b = span(j)
        src = (y + ny - p) % ny
        rcopy(ys.at[j, src, a:b], yr.at[j, src, a:b], y_ss.at[j, p], y_rs.at[j, p], yrow(p), c).wait_recv()

    def y_send(j):
        c_copy(j).wait_recv()
        for i, ref in mats(j):
            tot = ref[pl.ds(pl.multiple_of(co * half, half), half), :] + cr[j, i].astype(F32)
            tot = tot.reshape(ny, dc, w)
            tot = jnp.concatenate([tot[:, :, :w // 2], tot[:, :, w // 2:]], axis=1)
            ys[j, :, i] = tot.astype(BF)
        over(ny, lambda p: y_copy(j, p).start())
        for i, _ in mats(j):
            yr[j, y, i] = ys[j, y, i]

    def f_copy(k):
        return rcopy(fs.at[k], fr.at[c], f_ss.at[k], f_rs.at[c], row, plane_s(k, nz))

    def w_copy(k):
        return rcopy(fw.at[k], fv.at[c], w_ss.at[k], w_rs.at[c], row, plane_w(k, nz))

    def z_send(j):
        over(ny, lambda p: y_wait(j, p))
        for i, _ in mats(j):
            tot = yr[j, 0, i].astype(F32)
            for q in range(1, ny):
                tot = tot + yr[j, q, i].astype(F32)
            if i == 0:
                fw[j] = tot.astype(BF)
            else:
                fs[j - 1] = tot.astype(BF)
        if j < 4:
            @pl.when(c != plane_w(j, nz))
            def _():
                w_copy(j).start()

            @pl.when(c == plane_w(j, nz))
            def _():
                fv[c] = fw[j]
        if j > 0:
            @pl.when(c != plane_s(j - 1, nz))
            def _():
                f_copy(j - 1).start()

            @pl.when(c == plane_s(j - 1, nz))
            def _():
                fr[c] = fs[j - 1]

    def product(k):
        out = pv[k, c]
        for d in range(2):
            h = hops(k, d)
            if h > 0:
                rs_copy(k, d, h - 1).wait_recv()
                out = out + rsr[k, d, h - 1].astype(F32)
        return out

    def finish(k, carried):
        own_mask = pat[k, c * (ny * nx) + row].astype(F32)
        new = (-(product(k) + carried) * own_mask).astype(BF)
        nout[k] = new
        x_send(k, new)
        return new

    def early4():
        event(4)
        c_send(4)

    chain = {}

    def upper():
        chain[3] = finish(3, mm(topv[...], lv[3]))
        chain[2] = finish(2, mm(chain[3], lv[2]))
        z_send(4)

    hooks = {1: [early_sends], 2: [panels], 3: [d_terms], 4: [early4], 5: [panels_t, lambda: y_send(4)], 6: [upper]}
    for t in range(max(hi + 1, 7)):
        fresh = [k for k in (3, 2, 1, 0) if t == OFF[k]]
        if t == 0:
            for k in (3, 2):
                product_part(k)
            pl.semaphore_wait(bar, nc + (ny - 1) + (nz - 1))
        for k in fresh:
            if k < 2:
                product_part(k)
            rs_step(k, 0, 0)
            rs_step(k, 1, 0)
        for k in (3, 2, 1, 0):
            s = t - OFF[k]
            for d in range(2):
                if 0 < s < hops(k, d):
                    rs_step(k, d, s)
        for f in hooks.get(t, ()):
            f()
    n1 = finish(1, mm(chain[2], lv[1]))
    finish(0, mm(n1, lv[0]))
    out_n = pltpu.make_async_copy(nout, cols_h, out_sem.at[0])
    out_n.start()
    event(3)
    c_send(3)
    event(2)
    c_send(2)
    y_send(3)
    event(1)
    c_send(1)
    y_send(2)
    event(0)
    c_send(0)
    y_send(1)
    y_send(0)
    for s in range(hi):
        for k in range(SUP):
            for d in range(2):
                if s < hops(k, d):
                    rs_copy(k, d, s).wait_send()
    z_send(3)
    z_send(2)
    z_send(1)
    z_send(0)

    def from_plane(p):
        return (c + nz - p) % nz

    def g_copy(k, p):
        return rcopy(gs, ags.at[k], g_ss.at[p], g_rs.at[k], row, (c + p) % nz)

    def h_copy(k, p):
        return rcopy(gw, agw.at[k], h_ss.at[p], h_rs.at[k], row, (c + p) % nz)

    for k in range(SUP):
        @pl.when(c == plane_s(k, nz))
        def _():
            def f_wait(p):
                src = from_plane(p)
                rcopy(fs.at[k], fr.at[src], f_ss.at[k], f_rs.at[src], row, src).wait_recv()

            over(nz, f_wait)
            gs[...] = jnp.sum(fr[...].astype(F32), axis=0).astype(BF)
            over(nz, lambda p: g_copy(k, p).start())
            ags[k] = gs[...]

    for k in range(SUP):
        @pl.when(c == plane_w(k, nz))
        def _():
            def w_wait(p):
                src = from_plane(p)
                rcopy(fw.at[k], fv.at[src], w_ss.at[k], w_rs.at[src], row, src).wait_recv()

            over(nz, w_wait)
            gw[...] = jnp.sum(fv[...].astype(F32), axis=0).astype(BF)
            over(nz, lambda p: h_copy(k, p).start())
            agw[k] = gw[...]

    def drain_x(p):
        for j in range(5):
            x_copy(j, p).wait_send()
        d_copy(p).wait_send()

    def drain_y(p):
        for j in range(5):
            y_copy(j, p).wait_send()

    over(nc, drain_x)
    over(ny, drain_y)
    for j in range(5):
        c_copy(j).wait_send()

    for k in range(SUP):
        @pl.when(c != plane_s(k, nz))
        def _():
            f_copy(k).wait_send()
            g_copy(k, 1).wait_recv()

        @pl.when(c != plane_w(k, nz))
        def _():
            w_copy(k).wait_send()

    def take_p(k):
        @pl.when(c != plane_w(k, nz))
        def _():
            h_copy(k, 1).wait_recv()

        dout[k] = dv[k] + unfold(agw[k].astype(F32))

    for k in (3, 2, 1, 0):
        if k < 3:
            take_p(k + 1)
        prev = dout[k + 1] if k < 3 else dv[4]
        big = prev.astype(BF)
        small = (prev - big.astype(F32)).astype(BF)
        both = mm(jnp.concatenate([big, small], axis=0), lv[k])
        sout[k] = -(unfold(ags[k].astype(F32)) + both[:dc] + both[dc:])
    out_s = pltpu.make_async_copy(sout, sub_h, out_sem.at[2])
    out_d = pltpu.make_async_copy(dout.at[1:SUP], diag_h.at[1:SUP], out_sem.at[1])
    out_s.start()
    out_d.start()
    take_p(0)
    out_z = pltpu.make_async_copy(dout.at[0], diag_h.at[0], out_sem.at[3])
    out_z.start()

    for k in range(SUP):
        @pl.when(c == plane_w(k, nz))
        def _():
            over(nz, lambda p: h_copy(k, p).wait_send())

    for k in range(SUP):
        @pl.when(c == plane_s(k, nz))
        def _():
            over(nz, lambda p: g_copy(k, p).wait_send())

    out_n.wait()
    out_d.wait()
    out_s.wait()
    out_z.wait()


def hand_over(a, b, d, a_out, b_out, d_out, a_v, b_v, d_v, sem, sem_out):
    trips = ((a, a_v, a_out), (b, b_v, b_out), (d, d_v, d_out))
    loads = [pltpu.make_async_copy(src, mid, sem.at[i]) for i, (src, mid, _) in enumerate(trips)]
    stores = [pltpu.make_async_copy(mid, dst, sem_out.at[i]) for i, (_, mid, dst) in enumerate(trips)]
    for load in loads:
        load.start()
    for load, store in zip(loads, stores):
        load.wait()
        store.start()
    for store in stores:
        store.wait()


def local(known_inverse, lower_panel, chain_panel, diag_inverse, top_cols, top_diag, pattern):
    nr = lax.axis_size("rows")
    nz = lax.axis_size("cols")
    nx = 8 if nr >= 64 else 4
    ny = nr // nx
    pe = known_inverse.shape[2]
    w = lower_panel.shape[-1]
    dc = w // nr
    ub = nr * pe
    nc = nx // 2
    hi = nz // 2
    g = known_inverse.reshape(nz * pe, ub)
    m = lower_panel.reshape(SUP, ub, w)
    top = top_cols.reshape(pe, w)
    ku = nc * pe
    half = ny * dc
    dma = pltpu.SemaphoreType.DMA
    vm = pltpu.VMEM
    any_spec = pl.BlockSpec(memory_space=pltpu.HBM)
    scratch = [
        vm((nz * pe, ub), BF), vm((SUP, ub, w), BF), vm((SUP, w, w), BF), vm((SUP + 1, dc, w), F32),
        vm((pe, w), BF), vm((SUP, ub), F32), vm((SUP, nz, pe, w), F32),
        vm((SUP, 2, hi, pe, w), BF), vm((SUP, 2, hi, pe, w), BF),
        vm((5, nc, pe, w), BF), vm((nc, 4 * dc, w), BF), vm((10, ku, w), BF), vm((10, 2 * half, ku), BF),
        vm((SUP, 2 * half, w), F32), vm((SUP, 2 * half, w), F32),
        vm((5, 2, half, w), BF), vm((5, 2, half, w), BF),
        vm((5, ny, 2, 2 * dc, w // 2), BF), vm((5, ny, 2, 2 * dc, w // 2), BF),
        vm((SUP, 2 * dc, w // 2), BF), vm((nz, 2 * dc, w // 2), BF),
        vm((SUP, 2 * dc, w // 2), BF), vm((nz, 2 * dc, w // 2), BF),
        vm((2 * dc, w // 2), BF), vm((2 * dc, w // 2), BF),
        vm((SUP, 2 * dc, w // 2), BF), vm((SUP, 2 * dc, w // 2), BF),
        vm((SUP, pe, w), BF), vm((SUP, dc, w), F32), vm((SUP, dc, w), F32),
        dma((13,)), dma((4,)), dma((SUP, 2, hi)), dma((SUP, 2, hi)),
        dma((6, nc)), dma((6, nc)), dma((5,)), dma((5,)), dma((5, ny)), dma((5, ny)),
        dma((SUP,)), dma((nz,)), dma((SUP,)), dma((nz,)), dma((nz,)), dma((SUP,)), dma((nz,)), dma((SUP,)),
    ]
    outs = pl.pallas_call(
        functools.partial(kernel, nz, ny, nx),
        out_shape=(
            jax.ShapeDtypeStruct((SUP, pe, w), BF),
            jax.ShapeDtypeStruct((SUP, dc, w), F32),
            jax.ShapeDtypeStruct((SUP, dc, w), F32),
        ),
        in_specs=[any_spec] * 6 + [pl.BlockSpec(memory_space=pltpu.SMEM)],
        out_specs=(any_spec,) * 3,
        scratch_shapes=scratch,
        compiler_params=pltpu.CompilerParams(
            collective_id=0, has_side_effects=True, vmem_limit_bytes=64 * 1024 * 1024
        ),
        name="chain",
    )(g, m, chain_panel, diag_inverse, top, top_diag, pattern)
    cols, diag, sub = pl.pallas_call(
        hand_over,
        out_shape=tuple(jax.ShapeDtypeStruct(o.shape, o.dtype) for o in outs),
        in_specs=[any_spec] * 3,
        out_specs=(any_spec,) * 3,
        scratch_shapes=[vm(o.shape, o.dtype) for o in outs] + [dma((3,)), dma((3,))],
        name="hand_over",
    )(*outs)
    return cols.reshape(SUP, 1, 1, pe, w), diag, sub


def solution(mesh):
    in_specs = (
        P(None, "rows", None, "cols"),
        P(None, "cols", None, None, None),
        P(),
        P(None, "rows", None),
        P("cols", "rows", None, None),
        P("rows", None),
        P(),
    )
    out_specs = (P(None, "cols", "rows", None, None), P(None, "rows", None), P(None, "rows", None))
    return jax.shard_map(local, mesh=mesh, in_specs=in_specs, out_specs=out_specs, check_vma=False)
```
